32 devices in a mesh: groups: 2 (over y), patch: 4 (over z), sub: 2 (over x), half: 2 (over core).
Axes of the slice: x: 2, y: 2, z: 4, core: 2. Of those that a mesh axis runs over, the one named last changes fastest.
Arguments:
- vectors: float32 [2, 8192, 256], P(None, ('groups', 'patch', 'sub', 'half')), parts along dimension 1, may hold values from -600 to 600
- prestress: bfloat16 [8192, 3, 256], P(('groups', 'patch', 'sub', 'half')), parts along dimension 0, may hold values from -4 to 4
- thickness: float32 [8192, 256], P(('groups', 'patch', 'sub', 'half')), parts along dimension 0, may hold values from 0.5 to 2
- foundation: float32 [8192, 256], P(('groups', 'patch', 'sub', 'half')), parts along dimension 0, may hold values from 2 to 6
- patch_rows: int32 [64], P(('groups', 'patch', 'sub', 'half')), parts along dimension 0, may hold values from 64 to 128, as said below
- matched: int32 [64], P(('groups', 'patch', 'sub', 'half')), parts along dimension 0, may hold values from 0 to 31, as said below
- elem_row: int32 [8192], P(('groups', 'patch', 'sub', 'half')), parts along dimension 0, may hold values from 0 to 4095, as said below
Outputs:
- modes: float32 [2, 8192, 256], P(None, ('groups', 'patch', 'sub', 'half')), parts along dimension 1
The draws below stay inside these ranges and needn't reach their ends.
There are 2 independent parts, one for each index of `groups`. The reference program is written for one: setup_inputs(seed, part) draws one part's arguments, and reference() takes and returns one part's arrays. A program takes and returns all parts, laid end to end along the dimension named above; each array names one. Nothing has to cross between parts.
Inputs may be any that keep to these rules, and one draw needn't show every extreme that they name: `patch_rows`: the largest value is reached by some patch in every draw. A permutation of the patches; the patch matched to a patch lies on the device with the same sub and half indices and a patch index one above or one below, cyclically. `elem_row`: a permutation of the rows; of each device's rows, those in positions k * 16 to (k + 1) * 16 - 1 belong to patches of the device with index k along patch+sub+half.
All inputs are finite; a program needn't handle non-finite values.
Results may differ from the reference program's by a relative error of at most 0.0003.
Values may be sent and summed in bfloat16 or wider, within the bound.
A program may use at most 64 MiB of HBM per device.

```python
import math
import jax
import jax.numpy as jnp

PROWS = 128
C = 256
PSLOT = 2
ITERS = 2
PATCHES = 32
ROWS = 4096
N_PATCH = 4
N_SUB = 2
N_HALF = 2


def draw_vectors(key, part):
    first, second, third = jax.random.split(key, 3)
    row_scale = jnp.exp(jax.random.uniform(second, (2, ROWS, 1), jnp.float32, 0.0, math.log(10.0)))
    col_scale = jnp.exp(jax.random.uniform(third, (2, 1, C), jnp.float32, 0.0, math.log(10.0)))
    base = jnp.clip(jax.random.normal(first, (2, ROWS, C), jnp.float32), -6.0, 6.0)
    return base * row_scale * col_scale


def draw_patch_rows(key, part):
    first, second = jax.random.split(key)
    lengths = jax.random.randint(first, (PATCHES,), PROWS // 2, PROWS + 1).astype(jnp.int32)
    where_full = jax.random.randint(second, (), 0, PATCHES)
    return lengths.at[where_full].set(PROWS)


def draw_matched(key, part):
    groups_inner = N_SUB * N_HALF
    first, second = jax.random.split(key)
    direction = jax.random.randint(first, (groups_inner,), 0, 2).astype(jnp.int32) * 2 - 1
    direction = direction.at[0].set(1).at[1].set(-1)
    scores = jax.random.randint(second, (N_PATCH, groups_inner, PSLOT), 0, 2 ** 18).astype(jnp.int32) * PSLOT + jnp.arange(PSLOT, dtype=jnp.int32)
    slot_order = jnp.argsort(scores, axis=-1, stable=True).astype(jnp.int32)
    owner = jnp.arange(N_PATCH, dtype=jnp.int32)[:, None, None]
    inner = jnp.arange(groups_inner, dtype=jnp.int32)[None, :, None]
    target = (owner + direction[None, :, None]) % N_PATCH
    return ((target * groups_inner + inner) * PSLOT + slot_order).reshape(-1).astype(jnp.int32)


def draw_elem_row(key, part):
    devices_all = N_PATCH * N_SUB * N_HALF
    rows_dev = PSLOT * PROWS
    per_peer = rows_dev // devices_all
    scores = jax.random.randint(key, (devices_all, rows_dev), 0, 2 ** 18).astype(jnp.int32) * rows_dev + jnp.arange(rows_dev, dtype=jnp.int32)
    order = jnp.argsort(scores, axis=-1, stable=True).astype(jnp.int32)
    order = order.reshape(devices_all, devices_all, per_peer).transpose(1, 0, 2)
    owner = jnp.arange(devices_all, dtype=jnp.int32)[None, :, None]
    return (owner * rows_dev + order).reshape(-1).astype(jnp.int32)


def level_of(stream_key, extent, pieces, smallest, high):
    def one(axis_at, shards_of):
        steps = jax.random.uniform(jax.random.fold_in(jax.random.fold_in(stream_key, 6), axis_at), (shards_of,), jnp.float32, smallest / len(pieces), high / len(pieces))
        return jnp.repeat(jnp.exp(steps), extent[axis_at] // shards_of).reshape((-1,) + (1,) * (len(extent) - axis_at - 1))

    level = one(*pieces[0])
    for cut in pieces[1:]:
        level = level * one(*cut)
    return level


def noise(key, dims, scale, bound, cuts=(), held_as=jnp.bfloat16):
    level = level_of(key, dims, cuts, -0.22, 0.18) if cuts else 1.0
    result = jax.random.normal(key, dims, jnp.float32) * scale * level
    return jnp.minimum(jnp.maximum(result, -bound), bound).astype(held_as)


def setup_inputs(seed: int = 0, part: int = 0) -> dict:
    key_of = jax.random.split(jax.random.key(seed), 8)
    part_splits = jax.random.split(jax.random.fold_in(key_of[7], part), 8)
    vectors = draw_vectors(jax.random.fold_in(jax.random.fold_in(key_of[7], part), 71), part)
    prestress = noise(part_splits[1], (ROWS, 3, C), 1.0, 4.0, ((0, 16),))
    thickness = jnp.clip(jnp.exp(math.log(2.0) - 1.3862944 * jax.random.uniform(part_splits[2], (ROWS, C), jnp.float32) ** level_of(part_splits[2], (ROWS, C), ((0, 16),), -0.2, 0.2)), 0.5, 2.0)
    foundation = jnp.clip(jnp.exp(math.log(6.0) - 1.0986123 * jax.random.uniform(part_splits[3], (ROWS, C), jnp.float32) ** level_of(part_splits[3], (ROWS, C), ((0, 16),), -0.2, 0.2)), 2.0, 6.0)
    patch_rows = draw_patch_rows(jax.random.fold_in(jax.random.fold_in(key_of[7], part), 71), part)
    matched = draw_matched(jax.random.fold_in(jax.random.fold_in(key_of[7], part), 71), part)
    elem_row = draw_elem_row(jax.random.fold_in(jax.random.fold_in(key_of[7], part), 71), part)
    return {"vectors": vectors, "prestress": prestress, "thickness": thickness, "foundation": foundation, "patch_rows": patch_rows, "matched": matched, "elem_row": elem_row}


step_size = 1.0
norm_scale = 16.0
penalty_value = 8.0
penalty_slope = 4.0

def second_rows(field):
    padded = jnp.pad(field, [(0, 0)] * (field.ndim - 2) + [(1, 1), (0, 0)])
    return padded[..., :-2, :] - 2.0 * field + padded[..., 2:, :]

def second_cols(field):
    padded = jnp.pad(field, [(0, 0)] * (field.ndim - 1) + [(1, 1)])
    return padded[..., :-2] - 2.0 * field + padded[..., 2:]

def forward_rows(field):
    zeros = jnp.zeros_like(field[..., :1, :])
    return jnp.concatenate([field[..., 1:, :], zeros], axis=-2) - field

def backward_rows(field):
    zeros = jnp.zeros_like(field[..., :1, :])
    return jnp.concatenate([zeros, field[..., :-1, :]], axis=-2) - field

def forward_cols(field):
    zeros = jnp.zeros_like(field[..., :1])
    return jnp.concatenate([field[..., 1:], zeros], axis=-1) - field

def backward_cols(field):
    zeros = jnp.zeros_like(field[..., :1])
    return jnp.concatenate([zeros, field[..., :-1]], axis=-1) - field

def stiffness(field, live, thickness, foundation):
    bend_rows = thickness * live * second_rows(field)
    bend_cols = thickness * second_cols(field)
    return live * (foundation * field + second_rows(bend_rows) + second_cols(bend_cols))

def geometric(field, live, stress):
    along_rows = forward_rows(field)
    along_cols = forward_cols(field)
    nuu = stress[:, :, 0, :]
    nvv = stress[:, :, 1, :]
    nuv = stress[:, :, 2, :]
    total = backward_rows(nuu * along_rows + nuv * along_cols) + backward_cols(nvv * along_cols + nuv * along_rows)
    return live * total

def edges(field, lengths):

    def row_pick(index):
        where_rows = jnp.broadcast_to(index[None, :, None, None], (field.shape[0], field.shape[1], 1, field.shape[3]))
        return jnp.take_along_axis(field, where_rows, axis=2)[:, :, 0, :]
    top = jnp.stack([row_pick(lengths - 2), row_pick(lengths - 1)], axis=2)
    bottom = field[:, :, 0:2, :]
    return (top, bottom)

def interface(field, lengths, top, bottom, partner_top, partner_bottom):
    jump_top = top[:, :, 1, :] - partner_bottom[:, :, 0, :]
    slope_top = top[:, :, 1, :] - top[:, :, 0, :] - (partner_bottom[:, :, 1, :] - partner_bottom[:, :, 0, :])
    jump_bottom = partner_top[:, :, 1, :] - bottom[:, :, 0, :]
    slope_bottom = partner_top[:, :, 1, :] - partner_top[:, :, 0, :] - (bottom[:, :, 1, :] - bottom[:, :, 0, :])
    rows = jnp.arange(field.shape[2], dtype=jnp.int32)[None, :, None]
    last = lengths[:, None, None] - 1
    added = jnp.where(rows == last, (penalty_value * jump_top + penalty_slope * slope_top)[:, :, None, :], 0.0)
    added = added + jnp.where(rows == last - 1, (-penalty_slope * slope_top)[:, :, None, :], 0.0)
    added = added + jnp.where(rows == 0, (-penalty_value * jump_bottom + penalty_slope * slope_bottom)[:, :, None, :], 0.0)
    added = added + jnp.where(rows == 1, (-penalty_slope * slope_bottom)[:, :, None, :], 0.0)
    return added

def products(field, kfield, gfield):
    return jnp.stack([jnp.sum(field[0] * kfield[0]), jnp.sum(field[0] * kfield[1]), jnp.sum(field[1] * kfield[1]), jnp.sum(field[0] * gfield[0]), jnp.sum(field[0] * gfield[1]), jnp.sum(field[1] * gfield[1])])

def advance(field, kfield, gfield, totals, precond, cells):
    first_a = totals[0]
    cross_k = totals[1]
    second_a = totals[2]
    first_g = totals[3]
    cross_g = totals[4]
    second_g = totals[5]
    ratio = cross_k / first_a
    other = field[1] - ratio * field[0]
    other_k = kfield[1] - ratio * kfield[0]
    other_g = gfield[1] - ratio * gfield[0]
    other_a = second_a - ratio * cross_k
    other_q = second_g - 2.0 * ratio * cross_g + ratio * ratio * first_g
    first_mu = first_g / first_a
    other_mu = other_q / other_a
    new_first = (field[0] + step_size * precond * (gfield[0] - first_mu * kfield[0])) * jnp.sqrt(norm_scale * cells / first_a)
    new_other = (other + step_size * precond * (other_g - other_mu * other_k)) * jnp.sqrt(norm_scale * cells / other_a)
    return jnp.stack([new_first, new_other])

def reference(vectors, prestress, thickness, foundation, patch_rows, matched, elem_row):
    placed = jnp.zeros((ROWS, 3, C), jnp.bfloat16).at[elem_row].set(prestress)
    stress = placed.astype(jnp.float32).reshape(PATCHES, PROWS, 3, C)
    rows = jnp.arange(PROWS, dtype=jnp.int32)[None, :]
    live = (rows < patch_rows[:, None]).astype(jnp.float32)[:, :, None]
    thick = thickness.reshape(PATCHES, PROWS, C)
    support = foundation.reshape(PATCHES, PROWS, C)
    precond = live / (support + 12.0 * thick)
    inverse = jnp.zeros((PATCHES,), jnp.int32).at[matched].set(jnp.arange(PATCHES, dtype=jnp.int32))
    field = vectors.reshape(2, PATCHES, PROWS, C) * live
    cells = jnp.float32(ROWS * C)
    for step in range(ITERS):
        top, bottom = edges(field, patch_rows)
        partner_bottom = bottom[:, matched]
        partner_top = top[:, inverse]
        kfield = stiffness(field, live, thick, support) + interface(field, patch_rows, top, bottom, partner_top, partner_bottom)
        gfield = geometric(field, live, stress)
        totals = products(field, kfield, gfield)
        field = advance(field, kfield, gfield, totals, precond, cells)
    return field.reshape(2, ROWS, C)
```

```python
import jax
import jax.numpy as jnp
from jax import lax
from jax.experimental import pallas as pl
from jax.experimental.pallas import tpu as pltpu
from jax.sharding import PartitionSpec as P

step_size = 1.0
norm_scale = 16.0
penalty_value = 8.0
penalty_slope = 4.0

MESH = pl.DeviceIdType.MESH
PAD = 8
LANES = 128
TOTALS = 32
BAND = False


def body(
    vec, pre, thick_in, found_in, lengths_in, matched_in, elem, out,
    lengths, matched,
    x, v, w, mrow, frow, fside, thick, found, prec, stress, kf, gf, kv, fa, fb, fc, fd,
    colx, colv, rowx, rowv, seconds, nexts, backs, arrived, ids, onehot, strips, got, names, edge, reduced, sums, joints, coef,
    load_sem, own_sem, data_send, data_recv, ids_send, ids_recv,
    strip_send, strip_recv, name_send, name_recv, sum_send, sum_recv, joint_send, joint_recv,
):
    owners, subs, halves = (lax.axis_size(a) for a in ("patch", "sub", "half"))
    n = owners * subs * halves
    pi, si, hi = (lax.axis_index(a) for a in ("patch", "sub", "half"))
    me = (pi * subs + si) * halves + hi
    slots = x.shape[1]
    prows = x.shape[2] - 2 * PAD
    ncol = x.shape[3]
    rows_dev = slots * prows
    per_peer = rows_dev // n
    group = 2 * slots
    side = 2 * group
    cells = float(n * rows_dev * ncol)

    ends_of = 2 if owners % 2 == 0 else 1
    near = owners // ends_of

    def peer(d):
        step = lax.rem(d + (n // 2 if ends_of == 2 else 0), n)
        end = lax.rem(lax.div(pi, near) + lax.div(step, near * subs * halves), ends_of)
        along = lax.rem(lax.rem(pi, near) + lax.rem(lax.div(step, subs * halves), near), near)
        to_patch = end * near + along
        to_sub = lax.rem(si + lax.rem(lax.div(step, halves), subs), subs)
        to_half = lax.rem(hi + lax.rem(step, halves), halves)
        k = (to_patch * subs + to_sub) * halves + to_half
        return k, {"patch": to_patch, "sub": to_sub, "half": to_half}

    def for_peers(action):
        start = n // 2 if ends_of == 2 else 0

        def one(e):
            d = lax.select(e < start, e, e + 1) if start else e + 1
            action(*peer(d))

        if n <= 16:
            for e in range(n - 1):
                one(jnp.int32(e))
        else:
            pl.loop(0, n - 1)(one)

    barrier = pltpu.get_barrier_semaphore()

    def greet(k, where):
        pl.semaphore_signal(barrier, inc=1, device_id=where, device_id_type=MESH)

    for_peers(greet)

    def block_of(k):
        return lax.div(k * per_peer, LANES)

    loads = []
    for i in range(2):
        for s in range(slots):
            loads.append(
                pltpu.make_async_copy(
                    vec.at[i, pl.ds(s * prows, prows)],
                    x.at[i, s, pl.ds(PAD, prows)],
                    load_sem.at[i * slots + s],
                )
            )
    load_thick = pltpu.make_async_copy(thick_in, thick, load_sem.at[2 * slots])
    load_found = pltpu.make_async_copy(found_in, found, load_sem.at[2 * slots + 1])
    own_data = pltpu.make_async_copy(pre.at[:, me], arrived.at[:, me], own_sem.at[0])
    own_ids = pltpu.make_async_copy(elem.at[block_of(me)], ids.at[me], own_sem.at[1])
    load_ints = [
        pltpu.make_async_copy(lengths_in, lengths, own_sem.at[2]),
        pltpu.make_async_copy(matched_in, matched, own_sem.at[3]),
    ]
    for copy in load_ints + loads + [load_thick, load_found, own_data, own_ids]:
        copy.start()

    zero_pad = jnp.zeros((PAD, ncol), jnp.float32)
    for i in range(2):
        for s in range(slots):
            for ref in (x, v, w, mrow, frow, fside):
                ref[i, s, 0:PAD, :] = zero_pad
                ref[i, s, PAD + prows : 2 * PAD + prows, :] = zero_pad
    reduced[...] = jnp.zeros_like(reduced)
    for copy in load_ints + loads:
        copy.wait()

    def fill_strip(which, ref):
        for s in range(slots):
            length = jnp.maximum(lengths[s], 2)
            for i in range(2):
                at = i * slots + s
                last = ref[i, s, pl.ds(PAD + length - 1, 1), :]
                ahead = ref[i, s, pl.ds(PAD + length - 2, 1), :]
                first = ref[i, s, PAD : PAD + 1, :]
                second = ref[i, s, PAD + 1 : PAD + 2, :]
                strips[which, at : at + 1, :] = last
                strips[which, group + at : group + at + 1, :] = last - ahead
                strips[which, side + at : side + at + 1, :] = first
                strips[which, side + group + at : side + group + at + 1, :] = second - first

    fill_strip(0, x)
    label_lane = lax.broadcasted_iota(jnp.int32, (1, LANES), 1)
    label_row = jnp.zeros((1, LANES), jnp.int32)
    for s in range(slots):
        label_row = jnp.where(label_lane == s, matched[s], label_row)
    names[0] = label_row.astype(jnp.float32)

    def strip_copies(which, offsets):
        copies = []
        for d in offsets:
            at = which * (owners - 1) + d - 1
            copies.append(
                pltpu.make_async_remote_copy(
                    src_ref=strips.at[which],
                    dst_ref=got.at[which, d - 1],
                    send_sem=strip_send.at[at],
                    recv_sem=strip_recv.at[at],
                    device_id={"patch": lax.rem(pi + d, owners)},
                    device_id_type=MESH,
                )
            )
        return copies

    beside = sorted({1, owners - 1})
    everyone = range(1, owners)

    def send_block(k, where):
        pltpu.make_async_remote_copy(
            src_ref=elem.at[block_of(k)], dst_ref=ids.at[me], send_sem=ids_send.at[0],
            recv_sem=ids_recv.at[0], device_id=where, device_id_type=MESH,
        ).start()
        pltpu.make_async_remote_copy(
            src_ref=pre.at[:, k], dst_ref=arrived.at[:, me], send_sem=data_send.at[0],
            recv_sem=data_recv.at[0], device_id=where, device_id_type=MESH,
        ).start()

    def all_of(ref, send, recv):
        return pltpu.make_async_remote_copy(
            src_ref=ref, dst_ref=ref, send_sem=send, recv_sem=recv,
            device_id={"patch": pi}, device_id_type=MESH,
        )

    def all_ids():
        return all_of(ids.at[pl.ds(0, n - 1)], ids_send.at[0], ids_recv.at[0])

    def all_data():
        return all_of(arrived.at[:, pl.ds(0, n - 1)], data_send.at[0], data_recv.at[0])

    def all_sums():
        return all_of(sums.at[pl.ds(0, n - 1)], sum_send.at[0], sum_recv.at[0])

    chunk = prows
    first_lane = lax.broadcasted_iota(jnp.int32, (chunk, ncol), 1) == 0
    sub_row = lax.broadcasted_iota(jnp.int32, (chunk, ncol), 0)
    lane_row = lax.broadcasted_iota(jnp.int32, (ncol, ncol), 0)
    lane_col = lax.broadcasted_iota(jnp.int32, (ncol, ncol), 1)
    here = lane_row == lane_col

    def band(at_above, at_diagonal, at_below):
        value = jnp.where(here, at_diagonal, 0.0)
        value = jnp.where(lane_row == lane_col - 1, at_above, value)
        return jnp.where(lane_row == lane_col + 1, at_below, value).astype(jnp.bfloat16)

    for part in range(2):
        span = slice(part * ncol, (part + 1) * ncol)
        seconds[span, :] = band(1.0, -2.0, 1.0)
        nexts[span, :] = band(0.0, -1.0, 1.0)
        backs[span, :] = band(1.0, -1.0, 0.0)

    def columns(fields, *bands):
        halves = []
        for field in fields:
            high = field.astype(jnp.bfloat16)
            low = (field - high.astype(jnp.float32)).astype(jnp.bfloat16)
            halves.append(jnp.concatenate([high, low], axis=1))
        left = jnp.concatenate(halves, axis=0)
        results = []
        for ref in bands:
            both = jnp.dot(left, ref[...], preferred_element_type=jnp.float32)
            results.append([both[i * chunk : (i + 1) * chunk] for i in range(len(fields))])
        return results

    def rows(ref, i, s, r0, by=0):
        part = ref.at[i, s, pl.ds(r0, chunk + 2 * PAD)]
        return part[PAD + by : PAD + by + chunk, :]

    def place(ref, i, s, r0, value):
        ref[i, s, pl.ds(pl.multiple_of(r0 + PAD, 8), chunk), :] = value

    def flat(s, r0):
        return pl.ds(pl.multiple_of(s * prows + r0, chunk), chunk)

    def live_rows(s, r0):
        return r0 + sub_row < lengths[s]

    per_slot = prows // chunk

    def place_of(i):
        return lax.div(i, per_slot), pl.multiple_of(lax.rem(i, per_slot) * chunk, chunk)

    def for_chunks(action):
        @pl.loop(0, slots * per_slot, unroll=1)
        def _(i):
            action(*place_of(i))

    def sum_chunks(count, action):
        zero = jnp.zeros((8, LANES), jnp.float32)

        def one(i, acc):
            return tuple(a + fold(b) for a, b in zip(acc, action(*place_of(i))))

        return lax.fori_loop(0, slots * per_slot, one, (zero,) * count, unroll=1)

    def fold(value):
        half = value[:, 0:LANES]
        for j in range(LANES, ncol, LANES):
            half = half + value[:, j : j + LANES]
        total = half[0:8]
        for j in range(8, chunk, 8):
            total = total + half[j : j + 8]
        return total

    def put_totals(first, acc):
        for t, total in enumerate(acc, first):
            reduced[t : t + 1, :] = jnp.sum(total, axis=0, keepdims=True)

    def bend_rows(ref, s, r0):
        th = jnp.where(live_rows(s, r0), thick[flat(s, r0), :], 0.0)
        for i in range(2):
            a = rows(ref, i, s, r0)
            place(mrow, i, s, r0, th * (rows(ref, i, s, r0, -1) - 2.0 * a + rows(ref, i, s, r0, 1)))

    def stiff(fields, curved, s, r0):
        th, fo = thick[flat(s, r0), :], found[flat(s, r0), :]
        (bent,) = columns([th * c for c in curved], seconds)
        results = []
        for i in range(2):
            total = fo * fields[i] + bent[i] - 2.0 * rows(mrow, i, s, r0)
            results.append(total + (rows(mrow, i, s, r0, -1) + rows(mrow, i, s, r0, 1)))
        return results

    def turned_back(fields):
        if BAND:
            return columns(fields, backs)[0]
        return [jnp.where(first_lane, 0.0, pltpu.roll(f, 1, 1)) - f for f in fields]

    def geometric(aheads, along, s, r0, flows):
        nuu, nvv, nuv = (stress[c, flat(s, r0), :] for c in range(3))
        kept, across = [], []
        for i in range(2):
            flux = nuu * aheads[i] + nuv * along[i]
            place(flows, i, s, r0, flux)
            kept.append(flux)
            across.append(nvv * along[i] + nuv * aheads[i])
        back = turned_back(across)
        return [rows(flows, i, s, r0, -1) - kept[i] + back[i] for i in range(2)]

    def ahead_of(ref, fields, s, r0):
        return [rows(ref, i, s, r0, 1) - fields[i] for i in range(2)]

    def pair_of(ref, s, r0):
        return [rows(ref, i, s, r0) for i in range(2)]

    strip_row = lax.broadcasted_iota(jnp.int32, (side, ncol), 0)
    strip_slot = lax.rem(strip_row, slots)

    def turned(value, by):
        if by == 0:
            return value
        return jnp.where(
            strip_slot + by < slots,
            pltpu.roll(value, side - by, 0),
            pltpu.roll(value, slots - by, 0),
        )

    def strip_of(which, d):
        ref = strips.at[which] if d == 0 else got.at[which, d - 1]
        return ref[0:side, :], ref[side : 2 * side, :]

    def label_of(d):
        label = jnp.zeros((side, ncol), jnp.float32)
        for t in range(slots):
            one = names[d, :, t : t + 1]
            label = jnp.where(strip_slot == t, jnp.broadcast_to(one, (side, ncol)), label)
        return label

    def name_of(d, by):
        owner = lax.rem(pi - d + owners, owners)
        base = ((owner * subs + si) * halves + hi) * slots
        return (base + lax.rem(strip_slot + by, slots)).astype(jnp.float32)

    def beside_of(d):
        return sorted({(d + 1) % owners, (d + owners - 1) % owners})

    def jumps(which, d, label):
        total, _ = strip_of(which, d)
        for e in beside_of(d):
            for by in range(slots):
                hit = label == name_of(e, by)
                total = total - jnp.where(hit, turned(strip_of(which, e)[1], by), 0.0)
        return total

    def jumps_below(which, labels):
        total = -strip_of(which, 0)[1]
        for e in beside_of(0):
            for by in range(slots):
                hit = turned(labels[e], by) == name_of(0, 0)
                total = total + jnp.where(hit, turned(strip_of(which, e)[0], by), 0.0)
        return total

    def set_edges(to, above, below):
        edge[to, 0:group, :] = penalty_value * above[0:group] + penalty_slope * above[group:side]
        edge[to, group:side, :] = -penalty_slope * above[group:side]
        edge[to, side : side + group, :] = (
            penalty_slope * below[group:side] - penalty_value * below[0:group]
        )
        edge[to, side + group : 2 * side, :] = -penalty_slope * below[group:side]

    def joint(of, i, s, r0):
        row = r0 + sub_row
        length = lengths[s]
        at = i * slots + s

        def line(k):
            return edge[of, pl.ds(k * group + at, 1), :]

        total = jnp.where(row == length - 1, line(0), 0.0)
        total = jnp.where(row == length - 2, line(1), total)
        total = jnp.where(row == 0, line(2), total)
        return jnp.where(row == 1, line(3), total)

    load_thick.wait()
    load_found.wait()

    @for_chunks
    def _(s, r0):
        live = live_rows(s, r0)
        for i in range(2):
            place(x, i, s, r0, jnp.where(live, rows(x, i, s, r0), 0.0))
        at = flat(s, r0)
        prec[at, :] = jnp.where(live, step_size, 0.0) / (found[at, :] + 12.0 * thick[at, :])
        bend_rows(x, s, r0)

    pl.semaphore_wait(barrier, n - 1)

    first_strips = strip_copies(0, beside)
    name_copies = [
        pltpu.make_async_remote_copy(
            src_ref=names.at[0], dst_ref=names.at[d],
            send_sem=name_send.at[d - 1], recv_sem=name_recv.at[d - 1],
            device_id={"patch": lax.rem(pi + d, owners)}, device_id_type=MESH,
        )
        for d in everyone
    ]
    for copy in first_strips + name_copies:
        copy.start()
    for_peers(send_block)

    @for_chunks
    def _(s, r0):
        xs = pair_of(x, s, r0)
        curved, along = columns(xs, seconds, nexts)
        ks = stiff(xs, curved, s, r0)
        ahead = ahead_of(x, xs, s, r0)
        for i in range(2):
            colx[i, flat(s, r0), :] = along[i]
            rowx[i, flat(s, r0), :] = ahead[i]
            kf[i, flat(s, r0), :] = ks[i]

    for copy in first_strips + name_copies:
        copy.wait_recv()
    labels = {d: label_of(d) for d in [0] + beside}
    set_edges(0, jumps(0, 0, labels[0]), jumps_below(0, labels))

    def chunk_first(s, r0):
        at = flat(s, r0)
        ks = [kf[i, at, :] + joint(0, i, s, r0) for i in range(2)]
        vs = [prec[at, :] * k for k in ks]
        for i in range(2):
            kf[i, at, :] = ks[i]
            place(v, i, s, r0, vs[i])
        x0, x1 = pair_of(x, s, r0)
        return (
            x0 * ks[0], x0 * ks[1], x1 * ks[1],
            vs[0] * ks[0], vs[1] * ks[0], vs[0] * ks[1], vs[1] * ks[1],
        )

    acc_first = sum_chunks(7, chunk_first)
    fill_strip(1, v)

    def chunk_bent(s, r0):
        bend_rows(v, s, r0)
        vs = pair_of(v, s, r0)
        curved, along = columns(vs, seconds, nexts)
        ks = stiff(vs, curved, s, r0)
        ahead = ahead_of(v, vs, s, r0)
        for i in range(2):
            colv[i, flat(s, r0), :] = along[i]
            rowv[i, flat(s, r0), :] = ahead[i]
            kv[i, flat(s, r0), :] = ks[i]
        return vs[0] * ks[0], vs[0] * ks[1], vs[1] * ks[1]

    acc_bent = sum_chunks(3, chunk_bent)
    put_totals(0, acc_first[:3])
    put_totals(3, acc_bent)

    own_ids.wait()
    all_ids().wait_recv()
    who = jnp.broadcast_to(ids[...], (n, per_peer, LANES)).reshape(rows_dev, LANES)
    wide_lane = lax.broadcasted_iota(jnp.int32, (rows_dev, LANES), 1)
    wide_row = lax.broadcasted_iota(jnp.int32, (rows_dev, LANES), 0)
    pick = wide_lane == lax.rem(me * per_peer, LANES) + lax.rem(wide_row, per_peer)
    target = lax.rem(
        jnp.sum(jnp.where(pick, who, 0).astype(jnp.float32), axis=1, keepdims=True).astype(jnp.int32),
        rows_dev,
    )
    to = lax.broadcasted_iota(jnp.int32, (rows_dev, rows_dev), 1)
    onehot[...] = jnp.transpose((to == target).astype(jnp.float32)).astype(jnp.bfloat16)

    own_data.wait()
    all_data().wait_recv()
    second_strips = strip_copies(1, everyone)
    for copy in second_strips:
        copy.start()
    for c in range(3):
        block = arrived[c]
        if per_peer % 8:
            block = block.astype(jnp.float32).reshape(rows_dev, ncol).astype(jnp.bfloat16)
        else:
            block = block.reshape(rows_dev, ncol)
        stress[c] = jnp.dot(onehot[...], block, preferred_element_type=jnp.float32)

    def chunk_stress(s, r0):
        at = flat(s, r0)
        gs = geometric(*([ref[i, at, :] for i in range(2)] for ref in (rowx, colx)), s, r0, frow)
        for i in range(2):
            gf[i, at, :] = gs[i]
            place(w, i, s, r0, prec[at, :] * gs[i])
        x0, x1 = pair_of(x, s, r0)
        return x0 * gs[0], x0 * gs[1], x1 * gs[1]

    acc = sum_chunks(3, chunk_stress)
    fill_strip(2, w)
    third_strips = strip_copies(2, everyone)
    for copy in third_strips:
        copy.start()
    put_totals(6, acc)

    def chunk_second(s, r0):
        at = flat(s, r0)
        xs, ws, vs = (pair_of(ref, s, r0) for ref in (x, w, v))
        us = [xs[i] + ws[i] for i in range(2)]
        bend_rows(w, s, r0)
        curved, along = columns(ws, seconds, nexts)
        gw = geometric(ahead_of(w, ws, s, r0), along, s, r0, frow)
        gv = geometric(*([ref[i, at, :] for i in range(2)] for ref in (rowv, colv)), s, r0, fside)
        kw = stiff(ws, curved, s, r0)
        gs = [gf[i, at, :] for i in range(2)]
        ks = [kf[i, at, :] for i in range(2)]
        kvs = [kv[i, at, :] for i in range(2)]
        for i in range(2):
            fa[i, at, :] = gw[i]
            fb[i, at, :] = gv[i]
            fc[i, at, :] = kw[i]
        return (
            ws[0] * (2.0 * gs[0] + gw[0]),
            ws[0] * (gs[1] + gw[1]) + ws[1] * gs[0],
            ws[1] * (2.0 * gs[1] + gw[1]),
            us[0] * gv[0], us[0] * gv[1], us[1] * gv[0], us[1] * gv[1],
            vs[0] * gv[0], vs[0] * gv[1], vs[1] * gv[1],
            ws[0] * (2.0 * ks[0] + kw[0]),
            ws[0] * (ks[1] + kw[1]) + ws[1] * ks[0],
            ws[1] * (2.0 * ks[1] + kw[1]),
            ws[0] * kvs[0], ws[0] * kvs[1], ws[1] * kvs[0], ws[1] * kvs[1],
        )

    acc = sum_chunks(17, chunk_second)
    put_totals(9, acc[:13])
    put_totals(22, [a + b for a, b in zip(acc[13:], acc_first[3:])])

    spot = lax.broadcasted_iota(jnp.int32, (TOTALS, LANES), 1)
    spot_row = lax.broadcasted_iota(jnp.int32, (TOTALS, LANES), 0)
    each = jnp.sum(reduced[...], axis=1, keepdims=True)
    sums[me] = jnp.sum(jnp.where(spot == spot_row, each, 0.0), axis=0, keepdims=True)

    def send_line(k, where):
        pltpu.make_async_remote_copy(
            src_ref=sums.at[me], dst_ref=sums.at[me], send_sem=sum_send.at[0],
            recv_sem=sum_recv.at[0], device_id=where, device_id_type=MESH,
        ).start()

    for_peers(send_line)

    for copy in second_strips:
        copy.wait_recv()
    labels = {d: label_of(d) for d in range(owners)}
    v_jumps = [jumps(1, d, labels[d]) for d in range(owners)]
    set_edges(1, v_jumps[0], jumps_below(1, labels))
    for copy in third_strips:
        copy.wait_recv()
    weight = jnp.where(strip_row < group, penalty_value, penalty_slope)
    forms = None
    for d in range(owners):
        w_jump, v_jump = jumps(2, d, labels[d]), v_jumps[d]
        if d == 0:
            w_above = w_jump
        scaled = weight * w_jump
        scaled_v = weight * v_jump
        terms = [
            scaled * w_jump, scaled * pltpu.roll(w_jump, slots, 0),
            scaled * v_jump, scaled * pltpu.roll(v_jump, slots, 0),
            scaled * pltpu.roll(v_jump, side - slots, 0),
            scaled_v * v_jump, scaled_v * pltpu.roll(v_jump, slots, 0),
        ]
        forms = terms if forms is None else [a + b for a, b in zip(forms, terms)]
    half_rows = lax.rem(lax.broadcasted_iota(jnp.int32, (side, LANES), 0), group) < slots
    row_spot = lax.broadcasted_iota(jnp.int32, (1, LANES), 1)
    line = jnp.zeros((1, LANES), jnp.float32)
    for t, form, first in (
        (19, 0, True), (20, 1, False), (21, 0, False),
        (22, 2, True), (23, 4, True), (24, 3, False), (25, 2, False),
        (3, 5, True), (4, 6, False), (5, 5, False),
    ):
        value = forms[form][:, 0:LANES]
        for j in range(LANES, ncol, LANES):
            value = value + forms[form][:, j : j + LANES]
        value = jnp.where(half_rows, value, 0.0) if first else jnp.where(half_rows, 0.0, value)
        one = jnp.sum(jnp.sum(value, axis=0, keepdims=True), axis=1, keepdims=True)
        line = jnp.where(row_spot == t, one, line)
    inner = si * halves + hi
    joints[inner] = line
    joint_copies = []
    for e in range(1, subs * halves):
        joint_copies.append(
            pltpu.make_async_remote_copy(
                src_ref=joints.at[inner], dst_ref=joints.at[inner],
                send_sem=joint_send.at[e - 1], recv_sem=joint_recv.at[e - 1],
                device_id={
                    "sub": lax.rem(si + e // halves, subs), "half": lax.rem(hi + e % halves, halves)
                },
                device_id_type=MESH,
            )
        )
    for copy in joint_copies:
        copy.start()

    set_edges(2, w_above, jumps_below(2, labels))

    @for_chunks
    def _(s, r0):
        at = flat(s, r0)
        p = prec[at, :]
        for i in range(2):
            xi, wi, vi = (rows(ref, i, s, r0) for ref in (x, w, v))
            fa[i, at, :] = xi + 2.0 * wi + p * fa[i, at, :]
            fb[i, at, :] = vi + p * fb[i, at, :]
            fc[i, at, :] = vi + p * (fc[i, at, :] + joint(2, i, s, r0))
            fd[i, at, :] = p * (kv[i, at, :] + joint(1, i, s, r0))

    all_sums().wait_recv()
    line = jnp.sum(sums[...], axis=0)
    for copy in joint_copies:
        copy.wait_recv()
    line = line + jnp.sum(joints[...], axis=0)
    a1, c, a2, pk0, pk1, pk2, g1, h, g2, ug0, ug1, ug2, ug3, ug4, ug5, ug6, pg0, pg1, pg2, uk0, uk1, uk2, uk3, uk4, uk5, uk6 = (
        line[:, t : t + 1] for t in range(26)
    )

    uk0, uk1, uk2 = uk0 + a1, uk1 + c, uk2 + a2
    ug0, ug1, ug2 = ug0 + g1, ug1 + h, ug2 + g2

    def ratios(a1, c, a2, g1, h, g2):
        ratio = c / a1
        other_a = a2 - ratio * c
        other_q = g2 - 2.0 * ratio * h + ratio * ratio * g1
        return (
            ratio, g1 / a1, other_q / other_a,
            jnp.sqrt(norm_scale * cells / a1), jnp.sqrt(norm_scale * cells / other_a),
        )

    r, mu1, mu2, s0, s1 = ratios(a1, c, a2, g1, h, g2)

    def stepped(uu, uv, vv):
        uu0, uu1, uu2 = uu
        uv00, uv01, uv10, uv11 = uv
        vv0, vv1, vv2 = vv
        uu2 = uu2 - 2.0 * r * uu1 + r * r * uu0
        uu1 = uu1 - r * uu0
        uv11 = uv11 - r * (uv10 + uv01) + r * r * uv00
        uv01 = uv01 - r * uv00
        uv10 = uv10 - r * uv00
        vv2 = vv2 - 2.0 * r * vv1 + r * r * vv0
        vv1 = vv1 - r * vv0
        first = s0 * s0 * (uu0 - 2.0 * mu1 * uv00 + mu1 * mu1 * vv0)
        cross = s0 * s1 * (uu1 - mu2 * uv01 - mu1 * uv10 + mu1 * mu2 * vv1)
        second = s1 * s1 * (uu2 - 2.0 * mu2 * uv11 + mu2 * mu2 * vv2)
        return first, cross, second

    next_a = stepped((uk0, uk1, uk2), (uk3, uk4, uk5, uk6), (pk0, pk1, pk2))
    next_g = stepped((ug0, ug1, ug2), (ug3, ug4, ug5, ug6), (pg0, pg1, pg2))
    r2, nu1, nu2, t0, t1 = ratios(*next_a, *next_g)
    e1 = t0 * s0
    f1 = t1 * s1
    f5 = -t1 * (s1 * r + r2 * s0)
    f6 = t1 * (s1 * r * mu2 + r2 * s0 * mu1)
    values = (
        e1, -e1 * mu1, -e1 * nu1, e1 * mu1 * nu1,
        f1, -f1 * mu2, -f1 * nu2, f1 * mu2 * nu2,
        f5, f6, -nu2 * f5, -nu2 * f6,
    )
    for t, value in enumerate(values):
        coef[t : t + 1, :] = jnp.broadcast_to(value, (1, ncol))

    @for_chunks
    def _(s, r0):
        at = flat(s, r0)
        firsts = [ref[0, at, :] for ref in (fa, fb, fc, fd)]
        seconds = [ref[1, at, :] for ref in (fa, fb, fc, fd)]

        def mixed(first, fields):
            total = coef[first : first + 1, :] * fields[0]
            for t, field in enumerate(fields[1:], first + 1):
                total = total + coef[t : t + 1, :] * field
            return total

        out[0, at, :] = mixed(0, firsts)
        out[1, at, :] = mixed(4, seconds + firsts)


    for copy in first_strips + name_copies + second_strips + third_strips + joint_copies:
        copy.wait_send()
    all_ids().wait_send()
    all_data().wait_send()
    all_sums().wait_send()


def per_device(vectors, prestress, thickness, foundation, patch_rows, matched, elem_row):
    n = lax.axis_size(("patch", "sub", "half"))
    owners = lax.axis_size("patch")
    inner = n // owners
    slots = patch_rows.shape[0]
    rows_dev, ncol = thickness.shape
    prows = rows_dev // slots
    per_peer = rows_dev // n
    pre = jnp.transpose(prestress, (1, 0, 2)).reshape(3, n, per_peer, ncol)
    elem = elem_row.reshape(rows_dev // LANES, 1, LANES)
    f32 = jnp.float32
    padded = pltpu.VMEM((2, slots, prows + 2 * PAD, ncol), f32)
    flat = pltpu.VMEM((rows_dev, ncol), f32)
    pair = pltpu.VMEM((2, rows_dev, ncol), f32)
    side = 4 * slots
    hbm = pl.BlockSpec(memory_space=pltpu.HBM)
    dma = pltpu.SemaphoreType.DMA
    operands = (vectors, pre, thickness, foundation, patch_rows, matched, elem)
    return pl.pallas_call(
        body,
        out_shape=jax.ShapeDtypeStruct((2, rows_dev, ncol), f32),
        in_specs=[hbm] * 7,
        out_specs=pl.BlockSpec(memory_space=pltpu.VMEM),
        scratch_shapes=[
            pltpu.SMEM((slots,), jnp.int32), pltpu.SMEM((slots,), jnp.int32),
            padded, padded, padded, padded, padded, padded, flat, flat, flat,
            pltpu.VMEM((3, rows_dev, ncol), f32),
            pair, pair, pair, pair, pair, pair, pair, pair, pair, pair, pair,
            pltpu.VMEM((2 * ncol, ncol), jnp.bfloat16),
            pltpu.VMEM((2 * ncol, ncol), jnp.bfloat16),
            pltpu.VMEM((2 * ncol, ncol), jnp.bfloat16),
            pltpu.VMEM((3, n, per_peer, ncol), jnp.bfloat16),
            pltpu.VMEM((n, 1, LANES), jnp.int32),
            pltpu.VMEM((rows_dev, rows_dev), jnp.bfloat16),
            pltpu.VMEM((3, 2 * side, ncol), f32),
            pltpu.VMEM((3, owners - 1, 2 * side, ncol), f32),
            pltpu.VMEM((owners, 1, LANES), f32),
            pltpu.VMEM((3, 2 * side, ncol), f32),
            pltpu.VMEM((TOTALS, LANES), f32),
            pltpu.VMEM((n, 1, LANES), f32),
            pltpu.VMEM((inner, 1, LANES), f32),
            pltpu.VMEM((16, ncol), f32),
            dma((2 * slots + 2,)), dma((4,)),
            dma((1,)), dma((1,)), dma((1,)), dma((1,)),
            dma((3 * (owners - 1),)), dma((3 * (owners - 1),)),
            dma((owners - 1,)), dma((owners - 1,)),
            dma((1,)), dma((1,)), dma((inner - 1,)), dma((inner - 1,)),
        ],
        compiler_params=pltpu.CompilerParams(
            collective_id=0, has_side_effects=True, vmem_limit_bytes=32 << 20
        ),
    )(*(pltpu.with_memory_space_constraint(a, pltpu.HBM) for a in operands))


def solution(mesh):
    split = ("groups", "patch", "sub", "half")
    in_specs = (
        P(None, split, None),
        P(split, None, None),
        P(split, None),
        P(split, None),
        P(split),
        P(split),
        P(split),
    )
    return jax.shard_map(
        per_device, mesh=mesh, in_specs=in_specs, out_specs=P(None, split, None), check_vma=False
    )
```

```python
import jax
import jax.numpy as jnp
from jax import lax
from jax.experimental import pallas as pl
from jax.experimental.pallas import tpu as pltpu
from jax.sharding import PartitionSpec as P

step_size = 1.0
norm_scale = 16.0
penalty_value = 8.0
penalty_slope = 4.0

MESH = pl.DeviceIdType.MESH
PAD = 8
LANES = 128


def body(
    vec, pre, thick_in, found_in, lengths_in, matched_in, elem, fa, fb, fc, fd, coef,
    lengths, matched,
    x, v, w, mrow, frow, fside, thick, found, prec, stress, kf, gf, kv,
    colx, colv, rowx, rowv, seconds, nexts, arrived, ids, onehot, strips, got, high, got_high, low, got_low, names, edge, sums, joints,
    load_sem, own_sem, data_send, data_recv, ids_send, ids_recv,
    strip_send, strip_recv, high_send, high_recv, low_send, low_recv, name_send, name_recv, sum_send, sum_recv, joint_send, joint_recv,
):
    owners, subs, halves = (lax.axis_size(a) for a in ("patch", "sub", "half"))
    n = owners * subs * halves
    pi, si, hi = (lax.axis_index(a) for a in ("patch", "sub", "half"))
    me = (pi * subs + si) * halves + hi
    slots = x.shape[1]
    prows = x.shape[2] - 2 * PAD
    ncol = x.shape[3]
    rows_dev = slots * prows
    per_peer = rows_dev // n
    group = 2 * slots
    side = 2 * group
    cells = float(n * rows_dev * ncol)

    ends = 2 if owners % 2 == 0 else 1
    near = owners // ends
    inner = subs * halves

    def peer(end, along, rest):
        to_patch = lax.rem(lax.div(pi, near) + end, ends) * near + lax.rem(lax.rem(pi, near) + along, near)
        to_sub = lax.rem(si + lax.div(rest, halves), subs)
        to_half = lax.rem(hi + lax.rem(rest, halves), halves)
        k = (to_patch * subs + to_sub) * halves + to_half
        return k, {"patch": to_patch, "sub": to_sub, "half": to_half}

    def for_peers(action):
        def one(e):
            turn, rest = lax.div(e, inner), inner - 1 - lax.rem(e, inner)
            action(*peer(ends - 1 - lax.div(turn, near), near - 1 - lax.rem(turn, near) if ends == 1 else lax.rem(turn + 1, near), rest))

        if n <= 16:
            for end in range(ends - 1, -1, -1):
                for along in [*range(1, near), 0] if end == 0 else range(near):
                    for rest in range(inner - 1, -1, -1):
                        if end or along or rest:
                            action(*peer(end, along, rest))
        else:
            pl.loop(0, n - 1)(one)

    barrier = pltpu.get_barrier_semaphore()

    def greet(k, where):
        pl.semaphore_signal(barrier, inc=1, device_id=where, device_id_type=MESH)

    for_peers(greet)

    def block_of(k):
        return lax.div(k * per_peer, LANES)

    loads = []
    for i in range(2):
        for s in range(slots):
            loads.append(
                pltpu.make_async_copy(
                    vec.at[i, pl.ds(s * prows, prows)],
                    x.at[i, s, pl.ds(PAD, prows)],
                    load_sem.at[i * slots + s],
                )
            )
    load_thick = pltpu.make_async_copy(thick_in, thick, load_sem.at[2 * slots])
    load_found = pltpu.make_async_copy(found_in, found, load_sem.at[2 * slots + 1])
    own_data = pltpu.make_async_copy(pre.at[:, me], arrived.at[:, me], own_sem.at[0])
    own_ids = pltpu.make_async_copy(elem.at[block_of(me)], ids.at[me], own_sem.at[1])
    load_ints = [
        pltpu.make_async_copy(lengths_in, lengths, own_sem.at[2]),
        pltpu.make_async_copy(matched_in, matched, own_sem.at[3]),
    ]
    for copy in load_ints + loads + [load_thick, load_found, own_data, own_ids]:
        copy.start()

    zero_pad = jnp.zeros((PAD, ncol), jnp.float32)
    for i in range(2):
        for s in range(slots):
            for ref in (x, v, w, mrow, frow, fside):
                ref[i, s, 0:PAD, :] = zero_pad
                ref[i, s, PAD + prows : 2 * PAD + prows, :] = zero_pad
    for copy in load_ints + loads:
        copy.wait()

    def fill_strip(which, ref):
        for s in range(slots):
            length = jnp.maximum(lengths[s], 2)
            for i in range(2):
                at = i * slots + s
                last = ref[i, s, pl.ds(PAD + length - 1, 1), :]
                ahead = ref[i, s, pl.ds(PAD + length - 2, 1), :]
                first = ref[i, s, PAD : PAD + 1, :]
                second = ref[i, s, PAD + 1 : PAD + 2, :]
                strips[which, at : at + 1, :] = last
                strips[which, group + at : group + at + 1, :] = last - ahead
                strips[which, side + at : side + at + 1, :] = first
                strips[which, side + group + at : side + group + at + 1, :] = second - first

    fill_strip(0, x)
    label_lane = lax.broadcasted_iota(jnp.int32, (1, LANES), 1)
    label_row = jnp.zeros((1, LANES), jnp.int32)
    for s in range(slots):
        label_row = jnp.where(label_lane == s, matched[s], label_row)
    names[0] = label_row.astype(jnp.float32)

    def along_patch(ref, landing, send, recv, offsets):
        return [
            pltpu.make_async_remote_copy(
                src_ref=ref, dst_ref=landing.at[d - 1],
                send_sem=send.at[d - 1], recv_sem=recv.at[d - 1],
                device_id={"patch": lax.rem(pi + d, owners)}, device_id_type=MESH,
            )
            for d in offsets
        ]

    beside = sorted({1, owners - 1})
    everyone = range(1, owners)

    def send_block(k, where):
        pltpu.make_async_remote_copy(
            src_ref=elem.at[block_of(k)], dst_ref=ids.at[me], send_sem=ids_send.at[0],
            recv_sem=ids_recv.at[0], device_id=where, device_id_type=MESH,
        ).start()
        pltpu.make_async_remote_copy(
            src_ref=pre.at[:, k], dst_ref=arrived.at[:, me], send_sem=data_send.at[0],
            recv_sem=data_recv.at[0], device_id=where, device_id_type=MESH,
        ).start()

    def all_of(ref, send, recv):
        return pltpu.make_async_remote_copy(
            src_ref=ref, dst_ref=ref, send_sem=send, recv_sem=recv,
            device_id={"patch": pi}, device_id_type=MESH,
        )

    def all_ids():
        return all_of(ids.at[pl.ds(0, n - 1)], ids_send.at[0], ids_recv.at[0])

    def all_data():
        return all_of(arrived.at[:, pl.ds(0, n - 1)], data_send.at[0], data_recv.at[0])

    def all_sums():
        return all_of(sums.at[pl.ds(0, n - 1)], sum_send.at[0], sum_recv.at[0])

    chunk = prows
    first_lane = lax.broadcasted_iota(jnp.int32, (chunk, ncol), 1) == 0
    sub_row = lax.broadcasted_iota(jnp.int32, (chunk, ncol), 0)
    lane_row = lax.broadcasted_iota(jnp.int32, (ncol, ncol), 0)
    lane_col = lax.broadcasted_iota(jnp.int32, (ncol, ncol), 1)
    here = lane_row == lane_col

    def band(at_above, at_diagonal, at_below):
        value = jnp.where(here, at_diagonal, 0.0)
        value = jnp.where(lane_row == lane_col - 1, at_above, value)
        return jnp.where(lane_row == lane_col + 1, at_below, value).astype(jnp.bfloat16)

    for part in range(2):
        span = slice(part * ncol, (part + 1) * ncol)
        seconds[span, :] = band(1.0, -2.0, 1.0)
        nexts[span, :] = band(0.0, -1.0, 1.0)

    def columns(fields, *bands):
        halves = []
        for field in fields:
            high = field.astype(jnp.bfloat16)
            low = (field - high.astype(jnp.float32)).astype(jnp.bfloat16)
            halves.append(jnp.concatenate([high, low], axis=1))
        left = jnp.concatenate(halves, axis=0)
        results = []
        for ref in bands:
            both = jnp.dot(left, ref[...], preferred_element_type=jnp.float32)
            results.append([both[i * chunk : (i + 1) * chunk] for i in range(len(fields))])
        return results

    def rows(ref, i, s, r0, by=0):
        part = ref.at[i, s, pl.ds(r0, chunk + 2 * PAD)]
        return part[PAD + by : PAD + by + chunk, :]

    def place(ref, i, s, r0, value):
        ref[i, s, pl.ds(pl.multiple_of(r0 + PAD, 8), chunk), :] = value

    def flat(s, r0):
        return pl.ds(pl.multiple_of(s * prows + r0, chunk), chunk)

    def live_rows(s, r0):
        return r0 + sub_row < lengths[s]

    per_slot = prows // chunk

    def place_of(i):
        return lax.div(i, per_slot), pl.multiple_of(lax.rem(i, per_slot) * chunk, chunk)

    def for_chunks(action):
        @pl.loop(0, slots * per_slot, unroll=1)
        def _(i):
            action(*place_of(i))

    def sum_chunks(count, action):
        zero = jnp.zeros((8, LANES), jnp.float32)

        def one(i, acc):
            return tuple(a + fold(b) for a, b in zip(acc, action(*place_of(i))))

        return lax.fori_loop(0, slots * per_slot, one, (zero,) * count, unroll=1)

    def fold(value):
        half = value[:, 0:LANES]
        for j in range(LANES, ncol, LANES):
            half = half + value[:, j : j + LANES]
        total = half[0:8]
        for j in range(8, chunk, 8):
            total = total + half[j : j + 8]
        return total

    def to_line(values, spots):
        tall = jnp.concatenate(values, axis=0)
        pieces = []
        for _ in range(3):
            piece = tall.astype(jnp.bfloat16)
            tall = tall - piece.astype(jnp.float32)
            pieces.append(piece)
        ones = jnp.ones((3 * LANES, LANES), jnp.bfloat16)
        each = jnp.dot(jnp.concatenate(pieces, axis=1), ones, preferred_element_type=jnp.float32)
        spot = lax.broadcasted_iota(jnp.int32, (8, LANES), 1)
        total = jnp.zeros((8, LANES), jnp.float32)
        for k, t in enumerate(spots):
            total = total + jnp.where(spot == t, each[8 * k : 8 * k + 8], 0.0)
        return jnp.sum(total, axis=0, keepdims=True)

    def bend_rows(ref, s, r0):
        th = jnp.where(live_rows(s, r0), thick[flat(s, r0), :], 0.0)
        for i in range(2):
            a = rows(ref, i, s, r0)
            place(mrow, i, s, r0, th * (rows(ref, i, s, r0, -1) - 2.0 * a + rows(ref, i, s, r0, 1)))

    def stiff(fields, bends, s, r0):
        fo = found[flat(s, r0), :]
        (bent,) = columns(bends, seconds)
        results = []
        for i in range(2):
            total = fo * fields[i] + bent[i] - 2.0 * rows(mrow, i, s, r0)
            results.append(total + (rows(mrow, i, s, r0, -1) + rows(mrow, i, s, r0, 1)))
        return results

    def bends_of(curved, s, r0):
        th = thick[flat(s, r0), :]
        return [th * c for c in curved]

    def flows_of(aheads, along, s, r0, flows):
        nuu, nvv, nuv = (stress[c, flat(s, r0), :] for c in range(3))
        kept = [nuu * aheads[i] + nuv * along[i] for i in range(2)]
        for i in range(2):
            place(flows, i, s, r0, kept[i])
        return kept, [nvv * along[i] + nuv * aheads[i] for i in range(2)]

    def geometric(across, s, r0, flows):
        back = [jnp.where(first_lane, 0.0, pltpu.roll(f, 1, 1)) - f for f in across]
        return [rows(flows, i, s, r0, -1) - rows(flows, i, s, r0) + back[i] for i in range(2)]

    def ahead_of(ref, fields, s, r0):
        return [rows(ref, i, s, r0, 1) - fields[i] for i in range(2)]

    def both_of(ref, at):
        return [ref[i, at, :] for i in range(2)]

    def pair_of(ref, s, r0):
        return [rows(ref, i, s, r0) for i in range(2)]

    strip_row = lax.broadcasted_iota(jnp.int32, (side, ncol), 0)
    strip_slot = lax.rem(strip_row, slots)

    def turned(value, by):
        if by == 0:
            return value
        return jnp.where(
            strip_slot + by < slots,
            pltpu.roll(value, side - by, 0),
            pltpu.roll(value, slots - by, 0),
        )

    def strip_of(which, d, exact):
        if which and not exact:
            value = (high.at[which - 1] if d == 0 else got_high.at[which - 1, d - 1])[...].astype(jnp.float32)
        elif d == 0:
            value = strips[which]
        elif which == 0:
            value = got[d - 1]
        else:
            value = got_high[which - 1, d - 1].astype(jnp.float32) + got_low[which - 1, d - 1].astype(jnp.float32)
        return value[0:side], value[side : 2 * side]

    def round_strip(which):
        first = strips[which].astype(jnp.bfloat16)
        high[which - 1] = first
        low[which - 1] = (strips[which] - first.astype(jnp.float32)).astype(jnp.bfloat16)

    def label_of(d):
        label = jnp.zeros((side, ncol), jnp.float32)
        for t in range(slots):
            one = names[d, :, t : t + 1]
            label = jnp.where(strip_slot == t, jnp.broadcast_to(one, (side, ncol)), label)
        return label

    def name_of(d, by):
        owner = lax.rem(pi - d + owners, owners)
        base = ((owner * subs + si) * halves + hi) * slots
        return (base + lax.rem(strip_slot + by, slots)).astype(jnp.float32)

    def beside_of(d):
        return sorted({(d + 1) % owners, (d + owners - 1) % owners})

    def jumps(which, d, label, exact):
        total, _ = strip_of(which, d, exact)
        for e in beside_of(d):
            for by in range(slots):
                hit = label == name_of(e, by)
                total = total - jnp.where(hit, turned(strip_of(which, e, exact)[1], by), 0.0)
        return total

    def jumps_below(which, labels):
        total = -strip_of(which, 0, True)[1]
        for e in beside_of(0):
            for by in range(slots):
                hit = turned(labels[e], by) == name_of(0, 0)
                total = total + jnp.where(hit, turned(strip_of(which, e, True)[0], by), 0.0)
        return total

    def set_edges(to, above, below):
        edge[to, 0:group, :] = penalty_value * above[0:group] + penalty_slope * above[group:side]
        edge[to, group:side, :] = -penalty_slope * above[group:side]
        edge[to, side : side + group, :] = (
            penalty_slope * below[group:side] - penalty_value * below[0:group]
        )
        edge[to, side + group : 2 * side, :] = -penalty_slope * below[group:side]

    def joint(of, i, s, r0):
        row = r0 + sub_row
        length = lengths[s]
        at = i * slots + s

        def line(k):
            return edge[of, pl.ds(k * group + at, 1), :]

        total = jnp.where(row == length - 1, line(0), 0.0)
        total = jnp.where(row == length - 2, line(1), total)
        total = jnp.where(row == 0, line(2), total)
        return jnp.where(row == 1, line(3), total)

    load_thick.wait()
    load_found.wait()

    @for_chunks
    def _(s, r0):
        live = live_rows(s, r0)
        for i in range(2):
            place(x, i, s, r0, jnp.where(live, rows(x, i, s, r0), 0.0))
        at = flat(s, r0)
        prec[at, :] = jnp.where(live, step_size, 0.0) / (found[at, :] + 12.0 * thick[at, :])
        bend_rows(x, s, r0)

    pl.semaphore_wait(barrier, n - 1)

    first_strips = along_patch(strips.at[0], got, strip_send, strip_recv, beside)
    name_copies = along_patch(names.at[0], names.at[pl.ds(1, owners - 1)], name_send, name_recv, everyone)
    for copy in first_strips + name_copies:
        copy.start()
    for_peers(send_block)

    @for_chunks
    def _(s, r0):
        xs = pair_of(x, s, r0)
        curved, along = columns(xs, seconds, nexts)
        ks = stiff(xs, bends_of(curved, s, r0), s, r0)
        ahead = ahead_of(x, xs, s, r0)
        for i in range(2):
            colx[i, flat(s, r0), :] = along[i]
            rowx[i, flat(s, r0), :] = ahead[i]
            kf[i, flat(s, r0), :] = ks[i]

    for copy in first_strips + name_copies:
        copy.wait_recv()
    labels = {d: label_of(d) for d in [0] + beside}
    set_edges(0, jumps(0, 0, labels[0], True), jumps_below(0, labels))

    def chunk_first(s, r0):
        at = flat(s, r0)
        ks = [kf[i, at, :] + joint(0, i, s, r0) for i in range(2)]
        vs = [prec[at, :] * k for k in ks]
        for i in range(2):
            kf[i, at, :] = ks[i]
            place(v, i, s, r0, vs[i])
        x0, x1 = pair_of(x, s, r0)
        return (
            x0 * ks[0], x0 * ks[1], x1 * ks[1],
            vs[0] * ks[0], vs[1] * ks[0], vs[0] * ks[1], vs[1] * ks[1],
        )

    acc_first = sum_chunks(7, chunk_first)
    fill_strip(1, v)
    round_strip(1)

    def chunk_bent(s, r0):
        bend_rows(v, s, r0)
        vs = pair_of(v, s, r0)
        curved, along = columns(vs, seconds, nexts)
        ks = stiff(vs, bends_of(curved, s, r0), s, r0)
        ahead = ahead_of(v, vs, s, r0)
        for i in range(2):
            colv[i, flat(s, r0), :] = along[i]
            rowv[i, flat(s, r0), :] = ahead[i]
            kv[i, flat(s, r0), :] = ks[i]
        return vs[0] * ks[0], vs[0] * ks[1], vs[1] * ks[1]

    acc_bent = sum_chunks(3, chunk_bent)

    own_ids.wait()
    all_ids().wait_recv()
    who = jnp.broadcast_to(ids[...], (n, per_peer, LANES)).reshape(rows_dev, LANES)
    wide_lane = lax.broadcasted_iota(jnp.int32, (rows_dev, LANES), 1)
    wide_row = lax.broadcasted_iota(jnp.int32, (rows_dev, LANES), 0)
    pick = wide_lane == lax.rem(me * per_peer, LANES) + lax.rem(wide_row, per_peer)
    target = lax.rem(
        jnp.sum(jnp.where(pick, who, 0).astype(jnp.float32), axis=1, keepdims=True).astype(jnp.int32),
        rows_dev,
    )
    to = lax.broadcasted_iota(jnp.int32, (rows_dev, rows_dev), 1)
    onehot[...] = jnp.transpose((to == target).astype(jnp.float32)).astype(jnp.bfloat16)

    own_data.wait()
    all_data().wait_recv()
    second_strips = along_patch(high.at[0], got_high.at[0], high_send.at[0], high_recv.at[0], everyone)
    for copy in second_strips:
        copy.start()
    for c in range(3):
        block = arrived[c]
        if per_peer % 8:
            block = block.astype(jnp.float32).reshape(rows_dev, ncol).astype(jnp.bfloat16)
        else:
            block = block.reshape(rows_dev, ncol)
        stress[c] = jnp.dot(onehot[...], block, preferred_element_type=jnp.float32)

    def chunk_stress(s, r0):
        at = flat(s, r0)
        _, across = flows_of(*(both_of(ref, at) for ref in (rowx, colx)), s, r0, frow)
        gs = geometric(across, s, r0, frow)
        for i in range(2):
            gf[i, at, :] = gs[i]
            place(w, i, s, r0, prec[at, :] * gs[i])
        x0, x1 = pair_of(x, s, r0)
        return x0 * gs[0], x0 * gs[1], x1 * gs[1]

    acc_stress = sum_chunks(3, chunk_stress)
    fill_strip(2, w)
    round_strip(2)
    third_strips = along_patch(high.at[1], got_high.at[1], high_send.at[1], high_recv.at[1], everyone)
    low_strips = [
        copy
        for k in range(2)
        for copy in along_patch(low.at[k], got_low.at[k], low_send.at[k], low_recv.at[k], beside)
    ]
    for copy in third_strips + low_strips:
        copy.start()

    def chunk_second(s, r0):
        at = flat(s, r0)
        ws = pair_of(w, s, r0)
        curved, along = columns(ws, seconds, nexts)
        ahead = ahead_of(w, ws, s, r0)
        kept, across = flows_of(ahead, along, s, r0, frow)
        ahead_v, along_v = both_of(rowv, at), both_of(colv, at)
        kept_v, across_v = flows_of(ahead_v, along_v, s, r0, fside)
        bends = bends_of(curved, s, r0)
        fo = found[at, :]
        th = thick[at, :]
        live = live_rows(s, r0)
        arches = [rows(w, i, s, r0, -1) - 2.0 * ws[i] + rows(w, i, s, r0, 1) for i in range(2)]
        arch_live = [jnp.where(live, th * arch, 0.0) for arch in arches]
        for i in range(2):
            place(mrow, i, s, r0, arch_live[i])
            fa[i, at, :] = across[i]
            fb[i, at, :] = across_v[i]
            fc[i, at, :] = bends[i]
        gs, ks, kvs = both_of(gf, at), both_of(kf, at), both_of(kv, at)
        pairs = ((0, 0), (0, 1), (1, 1))
        squares = ((0, 0), (0, 1), (1, 0), (1, 1))
        held = [fo * field for field in ws]
        return (
            *(ws[i] * gs[j] for i, j in pairs),
            *(ws[i] * ks[j] for i, j in squares),
            *(ahead[i] * kept[j] + along[i] * across[j] for i, j in pairs),
            *(ahead_v[j] * kept[i] + along_v[j] * across[i] for i, j in squares),
            *(ahead_v[i] * kept_v[j] + along_v[i] * across_v[j] for i, j in pairs),
            *(held[i] * ws[j] + bends[i] * curved[j] + arch_live[i] * arches[j] for i, j in pairs),
            *(ws[i] * kvs[j] for i, j in squares),
        )

    acc = sum_chunks(24, chunk_second)
    last = [a + b for a, b in zip(acc[20:], acc_first[3:])]
    values = [*acc_first[:3], *acc_bent, *acc_stress, *acc[:20], *last]
    sums[me] = to_line(values, range(len(values)))

    def send_line(k, where):
        pltpu.make_async_remote_copy(
            src_ref=sums.at[me], dst_ref=sums.at[me], send_sem=sum_send.at[0],
            recv_sem=sum_recv.at[0], device_id=where, device_id_type=MESH,
        ).start()

    for_peers(send_line)

    for copy in second_strips:
        copy.wait_recv()
    labels = {d: label_of(d) for d in range(owners)}
    v_jumps = [jumps(1, d, labels[d], False) for d in range(owners)]
    for copy in third_strips:
        copy.wait_recv()
    weight = jnp.where(strip_row < group, penalty_value, penalty_slope)
    forms = None
    for d in range(owners):
        w_jump, v_jump = jumps(2, d, labels[d], False), v_jumps[d]
        scaled = weight * w_jump
        scaled_v = weight * v_jump
        terms = [
            scaled * w_jump, scaled * pltpu.roll(w_jump, slots, 0),
            scaled * v_jump, scaled * pltpu.roll(v_jump, slots, 0),
            scaled * pltpu.roll(v_jump, side - slots, 0),
            scaled_v * v_jump, scaled_v * pltpu.roll(v_jump, slots, 0),
        ]
        forms = terms if forms is None else [a + b for a, b in zip(forms, terms)]
    half_rows = lax.rem(lax.broadcasted_iota(jnp.int32, (side, LANES), 0), group) < slots
    spots, values = [], []
    for t, form, first in (
        (26, 0, True), (27, 1, False), (28, 0, False),
        (29, 2, True), (30, 4, True), (31, 3, False), (32, 2, False),
        (3, 5, True), (4, 6, False), (5, 5, False),
    ):
        value = forms[form][:, 0:LANES]
        for j in range(LANES, ncol, LANES):
            value = value + forms[form][:, j : j + LANES]
        spots.append(t)
        values.append(jnp.where(half_rows, value, 0.0) if first else jnp.where(half_rows, 0.0, value))
    line = to_line(values, spots)
    spot_of = si * halves + hi
    joints[spot_of] = line
    joint_copies = []
    for e in range(1, subs * halves):
        joint_copies.append(
            pltpu.make_async_remote_copy(
                src_ref=joints.at[spot_of], dst_ref=joints.at[spot_of],
                send_sem=joint_send.at[e - 1], recv_sem=joint_recv.at[e - 1],
                device_id={
                    "sub": lax.rem(si + e // halves, subs), "half": lax.rem(hi + e % halves, halves)
                },
                device_id_type=MESH,
            )
        )
    for copy in joint_copies:
        copy.start()

    for copy in low_strips:
        copy.wait_recv()
    for which in (1, 2):
        set_edges(which, jumps(which, 0, labels[0], True), jumps_below(which, labels))

    @for_chunks
    def _(s, r0):
        at = flat(s, r0)
        p = prec[at, :]
        xs, ws, vs = (pair_of(ref, s, r0) for ref in (x, w, v))
        kw = stiff(ws, both_of(fc, at), s, r0)
        gw = geometric(both_of(fa, at), s, r0, frow)
        gv = geometric(both_of(fb, at), s, r0, fside)
        for i in range(2):
            fa[i, at, :] = xs[i] + 2.0 * ws[i] + p * gw[i]
            fb[i, at, :] = vs[i] + p * gv[i]
            fc[i, at, :] = vs[i] + p * (kw[i] + joint(2, i, s, r0))
            fd[i, at, :] = p * (kv[i, at, :] + joint(1, i, s, r0))

    all_sums().wait_recv()
    line = jnp.sum(sums[...], axis=0)
    lanes = [line[:, t : t + 1] for t in range(33)]
    a1, c, a2, pk0, pk1, pk2, g1, h, g2 = lanes[:9]
    wg, wk, ww, wv, vv, kww = lanes[9:12], lanes[12:16], lanes[16:19], lanes[19:23], lanes[23:26], lanes[26:29]
    uk = (a1 + 2.0 * wk[0] + kww[0], c + wk[1] + wk[2] + kww[1], a2 + 2.0 * wk[3] + kww[2])
    ug = tuple(g + 2.0 * b + q for g, b, q in zip((g1, h, g2), wg, ww))
    mixed_g = tuple(b + q for b, q in zip(wk, wv))

    def ratios(a1, c, a2, g1, h, g2):
        ratio = c / a1
        other_a = a2 - ratio * c
        other_q = g2 - 2.0 * ratio * h + ratio * ratio * g1
        return (
            ratio, g1 / a1, other_q / other_a,
            jnp.sqrt(norm_scale * cells / a1), jnp.sqrt(norm_scale * cells / other_a),
        )

    r, mu1, mu2, s0, s1 = ratios(a1, c, a2, g1, h, g2)

    def stepped(uu, uv, vv):
        uu0, uu1, uu2 = uu
        uv00, uv01, uv10, uv11 = uv
        vv0, vv1, vv2 = vv
        uu2 = uu2 - 2.0 * r * uu1 + r * r * uu0
        uu1 = uu1 - r * uu0
        uv11 = uv11 - r * (uv10 + uv01) + r * r * uv00
        uv01 = uv01 - r * uv00
        uv10 = uv10 - r * uv00
        vv2 = vv2 - 2.0 * r * vv1 + r * r * vv0
        vv1 = vv1 - r * vv0
        first = s0 * s0 * (uu0 - 2.0 * mu1 * uv00 + mu1 * mu1 * vv0)
        cross = s0 * s1 * (uu1 - mu2 * uv01 - mu1 * uv10 + mu1 * mu2 * vv1)
        second = s1 * s1 * (uu2 - 2.0 * mu2 * uv11 + mu2 * mu2 * vv2)
        return first, cross, second

    next_g = stepped(ug, mixed_g, vv)
    next_a = stepped(uk, lanes[29:33], (pk0, pk1, pk2))
    for copy in joint_copies:
        copy.wait_recv()
    line = jnp.sum(joints[...], axis=0)
    parts = [line[:, t : t + 1] for t in (*range(26, 33), *range(3, 6))]
    next_a = tuple(a + b for a, b in zip(next_a, stepped(parts[:3], parts[3:7], parts[7:])))
    r2, nu1, nu2, t0, t1 = ratios(*next_a, *next_g)
    e1 = t0 * s0
    f1 = t1 * s1
    f5 = -t1 * (s1 * r + r2 * s0)
    f6 = t1 * (s1 * r * mu2 + r2 * s0 * mu1)
    values = (
        e1, -e1 * mu1, -e1 * nu1, e1 * mu1 * nu1,
        f1, -f1 * mu2, -f1 * nu2, f1 * mu2 * nu2,
        f5, f6, -nu2 * f5, -nu2 * f6,
    )
    for t, value in enumerate(values):
        coef[t : t + 1, :] = jnp.broadcast_to(value, (1, ncol))

    for copy in first_strips + name_copies + second_strips + third_strips + low_strips + joint_copies:
        copy.wait_send()
    all_ids().wait_send()
    all_data().wait_send()
    all_sums().wait_send()


def combine(fa, fb, fc, fd, coef, out, both, sem):
    rows_dev = fa.shape[1]
    piece = rows_dev // 8
    copies = []
    for k in range(8):
        at = pl.ds(k * piece, piece)
        firsts = [ref[0, at, :] for ref in (fa, fb, fc, fd)]
        seconds = [ref[1, at, :] for ref in (fa, fb, fc, fd)]

        def mixed(first, fields):
            total = coef[first : first + 1, :] * fields[0]
            for t, field in enumerate(fields[1:], first + 1):
                total = total + coef[t : t + 1, :] * field
            return total

        both[0, at, :] = mixed(0, firsts)
        both[1, at, :] = mixed(4, seconds + firsts)
        copy = pltpu.make_async_copy(both.at[:, at], out.at[:, at], sem.at[k])
        copy.start()
        copies.append(copy)
    for copy in copies:
        copy.wait()


def per_device(vectors, prestress, thickness, foundation, patch_rows, matched, elem_row):
    n = lax.axis_size(("patch", "sub", "half"))
    owners = lax.axis_size("patch")
    inner = n // owners
    slots = patch_rows.shape[0]
    rows_dev, ncol = thickness.shape
    prows = rows_dev // slots
    per_peer = rows_dev // n
    pre = jnp.transpose(prestress, (1, 0, 2)).reshape(3, n, per_peer, ncol)
    elem = elem_row.reshape(rows_dev // LANES, 1, LANES)
    f32 = jnp.float32
    padded = pltpu.VMEM((2, slots, prows + 2 * PAD, ncol), f32)
    flat = pltpu.VMEM((rows_dev, ncol), f32)
    pair = pltpu.VMEM((2, rows_dev, ncol), f32)
    side = 4 * slots
    hbm = pl.BlockSpec(memory_space=pltpu.HBM)
    dma = pltpu.SemaphoreType.DMA
    operands = (vectors, pre, thickness, foundation, patch_rows, matched, elem)
    in_vmem = pl.BlockSpec(memory_space=pltpu.VMEM)
    field = jax.ShapeDtypeStruct((2, rows_dev, ncol), f32)
    parts = pl.pallas_call(
        body,
        out_shape=[field] * 4 + [jax.ShapeDtypeStruct((16, ncol), f32)],
        in_specs=[hbm] * 7,
        out_specs=[in_vmem] * 5,
        scratch_shapes=[
            pltpu.SMEM((slots,), jnp.int32), pltpu.SMEM((slots,), jnp.int32),
            padded, padded, padded, padded, padded, padded, flat, flat, flat,
            pltpu.VMEM((3, rows_dev, ncol), f32),
            pair, pair, pair, pair, pair, pair, pair,
            pltpu.VMEM((2 * ncol, ncol), jnp.bfloat16),
            pltpu.VMEM((2 * ncol, ncol), jnp.bfloat16),
            pltpu.VMEM((3, n, per_peer, ncol), jnp.bfloat16),
            pltpu.VMEM((n, 1, LANES), jnp.int32),
            pltpu.VMEM((rows_dev, rows_dev), jnp.bfloat16),
            pltpu.VMEM((3, 2 * side, ncol), f32),
            pltpu.VMEM((owners - 1, 2 * side, ncol), f32),
            pltpu.VMEM((2, 2 * side, ncol), jnp.bfloat16),
            pltpu.VMEM((2, owners - 1, 2 * side, ncol), jnp.bfloat16),
            pltpu.VMEM((2, 2 * side, ncol), jnp.bfloat16),
            pltpu.VMEM((2, owners - 1, 2 * side, ncol), jnp.bfloat16),
            pltpu.VMEM((owners, 1, LANES), f32),
            pltpu.VMEM((3, 2 * side, ncol), f32),
            pltpu.VMEM((n, 1, LANES), f32),
            pltpu.VMEM((inner, 1, LANES), f32),
            dma((2 * slots + 2,)), dma((4,)),
            dma((1,)), dma((1,)), dma((1,)), dma((1,)),
            dma((owners - 1,)), dma((owners - 1,)),
            dma((2, owners - 1)), dma((2, owners - 1)),
            dma((2, owners - 1)), dma((2, owners - 1)),
            dma((owners - 1,)), dma((owners - 1,)),
            dma((1,)), dma((1,)), dma((inner - 1,)), dma((inner - 1,)),
        ],
        compiler_params=pltpu.CompilerParams(
            collective_id=0, has_side_effects=True, vmem_limit_bytes=32 << 20
        ),
    )(*(pltpu.with_memory_space_constraint(a, pltpu.HBM) for a in operands))
    return pl.pallas_call(
        combine,
        out_shape=field,
        in_specs=[in_vmem] * 5,
        out_specs=hbm,
        scratch_shapes=[pair, dma((8,))],
        compiler_params=pltpu.CompilerParams(vmem_limit_bytes=8 << 20),
    )(*parts)


def solution(mesh):
    split = ("groups", "patch", "sub", "half")
    in_specs = (
        P(None, split, None),
        P(split, None, None),
        P(split, None),
        P(split, None),
        P(split),
        P(split),
        P(split),
    )
    return jax.shard_map(
        per_device, mesh=mesh, in_specs=in_specs, out_specs=P(None, split, None), check_vma=False
    )
```

```python
import jax
import jax.numpy as jnp
from jax import lax
from jax.experimental import pallas as pl
from jax.experimental.pallas import tpu as pltpu
from jax.sharding import PartitionSpec as P

step_size = 1.0
norm_scale = 16.0
penalty_value = 8.0
penalty_slope = 4.0

MESH = pl.DeviceIdType.MESH
PAD = 8
LANES = 128


def body(
    vec, pre, thick_in, found_in, lengths_in, matched_in, elem, fa, fb, fc, fd, coef,
    lengths, matched,
    x, v, w, mrow, frow, fside, thick, found, prec, stress, kf, gf, kv,
    colx, colv, rowx, rowv, seconds, nexts, arrived, ids, onehot, strips, got, high, got_high, low, got_low, names, edge, sums, joints,
    load_sem, own_sem, data_send, data_recv, ids_send, ids_recv,
    strip_send, strip_recv, high_send, high_recv, low_send, low_recv, name_send, name_recv, sum_send, sum_recv, joint_send, joint_recv,
):
    owners, subs, halves = (lax.axis_size(a) for a in ("patch", "sub", "half"))
    n = owners * subs * halves
    pi, si, hi = (lax.axis_index(a) for a in ("patch", "sub", "half"))
    me = (pi * subs + si) * halves + hi
    slots = x.shape[1]
    prows = x.shape[2] - 2 * PAD
    ncol = x.shape[3]
    rows_dev = slots * prows
    per_peer = rows_dev // n
    group = 2 * slots
    side = 2 * group
    cells = float(n * rows_dev * ncol)

    ends = 2 if owners % 2 == 0 else 1
    near = owners // ends
    inner = subs * halves

    def peer(end, along, rest):
        to_patch = lax.rem(lax.div(pi, near) + end, ends) * near + lax.rem(lax.rem(pi, near) + along, near)
        to_sub = lax.rem(si + lax.div(rest, halves), subs)
        to_half = lax.rem(hi + lax.rem(rest, halves), halves)
        k = (to_patch * subs + to_sub) * halves + to_half
        return k, {"patch": to_patch, "sub": to_sub, "half": to_half}

    def for_peers(action):
        def one(e):
            turn, rest = lax.div(e, inner), inner - 1 - lax.rem(e, inner)
            action(*peer(ends - 1 - lax.div(turn, near), near - 1 - lax.rem(turn, near) if ends == 1 else lax.rem(turn + 1, near), rest))

        if n <= 16:
            for end in range(ends - 1, -1, -1):
                for along in [*range(1, near), 0] if end == 0 else range(near):
                    for rest in range(inner - 1, -1, -1):
                        if end or along or rest:
                            action(*peer(end, along, rest))
        else:
            pl.loop(0, n - 1)(one)

    barrier = pltpu.get_barrier_semaphore()

    def greet(k, where):
        pl.semaphore_signal(barrier, inc=1, device_id=where, device_id_type=MESH)

    for_peers(greet)

    def block_of(k):
        return lax.div(k * per_peer, LANES)

    loads = []
    for i in range(2):
        for s in range(slots):
            loads.append(
                pltpu.make_async_copy(
                    vec.at[i, pl.ds(s * prows, prows)],
                    x.at[i, s, pl.ds(PAD, prows)],
                    load_sem.at[i * slots + s],
                )
            )
    load_thick = pltpu.make_async_copy(thick_in, thick, load_sem.at[2 * slots])
    load_found = pltpu.make_async_copy(found_in, found, load_sem.at[2 * slots + 1])
    own_data = pltpu.make_async_copy(pre.at[:, me], arrived.at[:, me], own_sem.at[0])
    own_ids = pltpu.make_async_copy(elem.at[block_of(me)], ids.at[me], own_sem.at[1])
    load_ints = [
        pltpu.make_async_copy(lengths_in, lengths, own_sem.at[2]),
        pltpu.make_async_copy(matched_in, matched, own_sem.at[3]),
    ]
    for copy in load_ints + loads + [load_thick, load_found, own_data, own_ids]:
        copy.start()

    zero_pad = jnp.zeros((PAD, ncol), jnp.float32)
    for i in range(2):
        for s in range(slots):
            for ref in (x, v, w, mrow, frow, fside):
                ref[i, s, 0:PAD, :] = zero_pad
                ref[i, s, PAD + prows : 2 * PAD + prows, :] = zero_pad
    for copy in load_ints + loads:
        copy.wait()

    def fill_strip(which, ref):
        for s in range(slots):
            length = jnp.maximum(lengths[s], 2)
            for i in range(2):
                at = i * slots + s
                last = ref[i, s, pl.ds(PAD + length - 1, 1), :]
                ahead = ref[i, s, pl.ds(PAD + length - 2, 1), :]
                first = ref[i, s, PAD : PAD + 1, :]
                second = ref[i, s, PAD + 1 : PAD + 2, :]
                strips[which, at : at + 1, :] = last
                strips[which, group + at : group + at + 1, :] = last - ahead
                strips[which, side + at : side + at + 1, :] = first
                strips[which, side + group + at : side + group + at + 1, :] = second - first

    fill_strip(0, x)
    label_lane = lax.broadcasted_iota(jnp.int32, (1, LANES), 1)
    label_row = jnp.zeros((1, LANES), jnp.int32)
    for s in range(slots):
        label_row = jnp.where(label_lane == s, matched[s], label_row)
    names[0] = label_row.astype(jnp.float32)

    def along_patch(ref, landing, send, recv, offsets):
        return [
            pltpu.make_async_remote_copy(
                src_ref=ref, dst_ref=landing.at[d - 1],
                send_sem=send.at[d - 1], recv_sem=recv.at[d - 1],
                device_id={"patch": lax.rem(pi + d, owners)}, device_id_type=MESH,
            )
            for d in offsets
        ]

    beside = sorted({1, owners - 1})
    everyone = range(1, owners)

    def send_block(k, where):
        pltpu.make_async_remote_copy(
            src_ref=elem.at[block_of(k)], dst_ref=ids.at[me], send_sem=ids_send.at[0],
            recv_sem=ids_recv.at[0], device_id=where, device_id_type=MESH,
        ).start()
        pltpu.make_async_remote_copy(
            src_ref=pre.at[:, k], dst_ref=arrived.at[:, me], send_sem=data_send.at[0],
            recv_sem=data_recv.at[0], device_id=where, device_id_type=MESH,
        ).start()

    def all_of(ref, send, recv):
        return pltpu.make_async_remote_copy(
            src_ref=ref, dst_ref=ref, send_sem=send, recv_sem=recv,
            device_id={"patch": pi}, device_id_type=MESH,
        )

    def all_ids():
        return all_of(ids.at[pl.ds(0, n - 1)], ids_send.at[0], ids_recv.at[0])

    def all_data():
        return all_of(arrived.at[:, pl.ds(0, n - 1)], data_send.at[0], data_recv.at[0])

    def all_sums():
        return all_of(sums.at[pl.ds(0, n - 1)], sum_send.at[0], sum_recv.at[0])

    chunk = prows
    first_lane = lax.broadcasted_iota(jnp.int32, (chunk, ncol), 1) == 0
    sub_row = lax.broadcasted_iota(jnp.int32, (chunk, ncol), 0)
    lane_row = lax.broadcasted_iota(jnp.int32, (ncol, ncol), 0)
    lane_col = lax.broadcasted_iota(jnp.int32, (ncol, ncol), 1)
    here = lane_row == lane_col

    def band(at_above, at_diagonal, at_below):
        value = jnp.where(here, at_diagonal, 0.0)
        value = jnp.where(lane_row == lane_col - 1, at_above, value)
        return jnp.where(lane_row == lane_col + 1, at_below, value).astype(jnp.bfloat16)

    for part in range(2):
        span = slice(part * ncol, (part + 1) * ncol)
        seconds[span, :] = band(1.0, -2.0, 1.0)
        nexts[span, :] = band(0.0, -1.0, 1.0)

    def columns(fields, *bands):
        halves = []
        for field in fields:
            high = field.astype(jnp.bfloat16)
            low = (field - high.astype(jnp.float32)).astype(jnp.bfloat16)
            halves.append(jnp.concatenate([high, low], axis=1))
        left = jnp.concatenate(halves, axis=0)
        results = []
        for ref in bands:
            both = jnp.dot(left, ref[...], preferred_element_type=jnp.float32)
            results.append([both[i * chunk : (i + 1) * chunk] for i in range(len(fields))])
        return results

    def rows(ref, i, s, r0, by=0):
        part = ref.at[i, s, pl.ds(r0, chunk + 2 * PAD)]
        return part[PAD + by : PAD + by + chunk, :]

    def place(ref, i, s, r0, value):
        ref[i, s, pl.ds(pl.multiple_of(r0 + PAD, 8), chunk), :] = value

    def flat(s, r0):
        return pl.ds(pl.multiple_of(s * prows + r0, chunk), chunk)

    def live_rows(s, r0):
        return r0 + sub_row < lengths[s]

    per_slot = prows // chunk

    def place_of(i):
        return lax.div(i, per_slot), pl.multiple_of(lax.rem(i, per_slot) * chunk, chunk)

    def for_chunks(action):
        @pl.loop(0, slots * per_slot, unroll=1)
        def _(i):
            action(*place_of(i))

    def sum_chunks(count, action):
        zero = jnp.zeros((8, LANES), jnp.float32)

        def one(i, acc):
            return tuple(a + fold(b) for a, b in zip(acc, action(*place_of(i))))

        return lax.fori_loop(0, slots * per_slot, one, (zero,) * count, unroll=1)

    def fold(value):
        half = value[:, 0:LANES]
        for j in range(LANES, ncol, LANES):
            half = half + value[:, j : j + LANES]
        total = half[0:8]
        for j in range(8, chunk, 8):
            total = total + half[j : j + 8]
        return total

    def to_line(values, spots):
        tall = jnp.concatenate(values, axis=0)
        pieces = []
        for _ in range(3):
            piece = tall.astype(jnp.bfloat16)
            tall = tall - piece.astype(jnp.float32)
            pieces.append(piece)
        ones = jnp.ones((3 * LANES, LANES), jnp.bfloat16)
        each = jnp.dot(jnp.concatenate(pieces, axis=1), ones, preferred_element_type=jnp.float32)
        spot = lax.broadcasted_iota(jnp.int32, (8, LANES), 1)
        total = jnp.zeros((8, LANES), jnp.float32)
        for k, t in enumerate(spots):
            total = total + jnp.where(spot == t, each[8 * k : 8 * k + 8], 0.0)
        return jnp.sum(total, axis=0, keepdims=True)

    def bend_rows(ref, s, r0):
        th = jnp.where(live_rows(s, r0), thick[flat(s, r0), :], 0.0)
        for i in range(2):
            a = rows(ref, i, s, r0)
            place(mrow, i, s, r0, th * (rows(ref, i, s, r0, -1) - 2.0 * a + rows(ref, i, s, r0, 1)))

    def stiff(fields, bends, s, r0):
        fo = found[flat(s, r0), :]
        (bent,) = columns(bends, seconds)
        results = []
        for i in range(2):
            total = fo * fields[i] + bent[i] - 2.0 * rows(mrow, i, s, r0)
            results.append(total + (rows(mrow, i, s, r0, -1) + rows(mrow, i, s, r0, 1)))
        return results

    def bends_of(curved, s, r0):
        th = thick[flat(s, r0), :]
        return [th * c for c in curved]

    def flows_of(aheads, along, s, r0, flows):
        nuu, nvv, nuv = (stress[c, flat(s, r0), :] for c in range(3))
        kept = [nuu * aheads[i] + nuv * along[i] for i in range(2)]
        for i in range(2):
            place(flows, i, s, r0, kept[i])
        return kept, [nvv * along[i] + nuv * aheads[i] for i in range(2)]

    def geometric(across, s, r0, flows):
        back = [jnp.where(first_lane, 0.0, pltpu.roll(f, 1, 1)) - f for f in across]
        return [rows(flows, i, s, r0, -1) - rows(flows, i, s, r0) + back[i] for i in range(2)]

    def ahead_of(ref, fields, s, r0):
        return [rows(ref, i, s, r0, 1) - fields[i] for i in range(2)]

    def both_of(ref, at):
        return [ref[i, at, :] for i in range(2)]

    def pair_of(ref, s, r0):
        return [rows(ref, i, s, r0) for i in range(2)]

    strip_row = lax.broadcasted_iota(jnp.int32, (side, ncol), 0)
    strip_slot = lax.rem(strip_row, slots)

    def turned(value, by):
        if by == 0:
            return value
        return jnp.where(
            strip_slot + by < slots,
            pltpu.roll(value, side - by, 0),
            pltpu.roll(value, slots - by, 0),
        )

    def strip_of(which, d, exact):
        if which and not exact:
            value = (high.at[which - 1] if d == 0 else got_high.at[which - 1, d - 1])[...].astype(jnp.float32)
        elif d == 0:
            value = strips[which]
        elif which == 0:
            value = got[d - 1]
        else:
            value = got_high[which - 1, d - 1].astype(jnp.float32) + got_low[which - 1, d - 1].astype(jnp.float32)
        return value[0:side], value[side : 2 * side]

    def round_strip(which):
        first = strips[which].astype(jnp.bfloat16)
        high[which - 1] = first
        low[which - 1] = (strips[which] - first.astype(jnp.float32)).astype(jnp.bfloat16)

    def label_of(d):
        label = jnp.zeros((side, ncol), jnp.float32)
        for t in range(slots):
            one = names[d, :, t : t + 1]
            label = jnp.where(strip_slot == t, jnp.broadcast_to(one, (side, ncol)), label)
        return label

    def name_of(d, by):
        owner = lax.rem(pi - d + owners, owners)
        base = ((owner * subs + si) * halves + hi) * slots
        return (base + lax.rem(strip_slot + by, slots)).astype(jnp.float32)

    def beside_of(d):
        return sorted({(d + 1) % owners, (d + owners - 1) % owners})

    def jumps(which, d, label, exact):
        total, _ = strip_of(which, d, exact)
        for e in beside_of(d):
            for by in range(slots):
                hit = label == name_of(e, by)
                total = total - jnp.where(hit, turned(strip_of(which, e, exact)[1], by), 0.0)
        return total

    def jumps_below(which, labels):
        total = -strip_of(which, 0, True)[1]
        for e in beside_of(0):
            for by in range(slots):
                hit = turned(labels[e], by) == name_of(0, 0)
                total = total + jnp.where(hit, turned(strip_of(which, e, True)[0], by), 0.0)
        return total

    def set_edges(to, above, below):
        edge[to, 0:group, :] = penalty_value * above[0:group] + penalty_slope * above[group:side]
        edge[to, group:side, :] = -penalty_slope * above[group:side]
        edge[to, side : side + group, :] = (
            penalty_slope * below[group:side] - penalty_value * below[0:group]
        )
        edge[to, side + group : 2 * side, :] = -penalty_slope * below[group:side]

    def joint(of, i, s, r0):
        row = r0 + sub_row
        length = lengths[s]
        at = i * slots + s

        def line(k):
            return edge[of, pl.ds(k * group + at, 1), :]

        total = jnp.where(row == length - 1, line(0), 0.0)
        total = jnp.where(row == length - 2, line(1), total)
        total = jnp.where(row == 0, line(2), total)
        return jnp.where(row == 1, line(3), total)

    load_thick.wait()
    load_found.wait()

    @for_chunks
    def _(s, r0):
        live = live_rows(s, r0)
        for i in range(2):
            place(x, i, s, r0, jnp.where(live, rows(x, i, s, r0), 0.0))
        at = flat(s, r0)
        prec[at, :] = jnp.where(live, step_size, 0.0) / (found[at, :] + 12.0 * thick[at, :])
        bend_rows(x, s, r0)

    pl.semaphore_wait(barrier, n - 1)

    first_strips = along_patch(strips.at[0], got, strip_send, strip_recv, beside)
    name_copies = along_patch(names.at[0], names.at[pl.ds(1, owners - 1)], name_send, name_recv, everyone)
    for copy in first_strips + name_copies:
        copy.start()
    for_peers(send_block)

    @for_chunks
    def _(s, r0):
        xs = pair_of(x, s, r0)
        curved, along = columns(xs, seconds, nexts)
        ks = stiff(xs, bends_of(curved, s, r0), s, r0)
        ahead = ahead_of(x, xs, s, r0)
        for i in range(2):
            colx[i, flat(s, r0), :] = along[i]
            rowx[i, flat(s, r0), :] = ahead[i]
            kf[i, flat(s, r0), :] = ks[i]

    for copy in first_strips + name_copies:
        copy.wait_recv()
    labels = {d: label_of(d) for d in [0] + beside}
    set_edges(0, jumps(0, 0, labels[0], True), jumps_below(0, labels))

    def chunk_first(s, r0):
        at = flat(s, r0)
        ks = [kf[i, at, :] + joint(0, i, s, r0) for i in range(2)]
        vs = [prec[at, :] * k for k in ks]
        for i in range(2):
            kf[i, at, :] = ks[i]
            place(v, i, s, r0, vs[i])
        x0, x1 = pair_of(x, s, r0)
        return (
            x0 * ks[0], x0 * ks[1], x1 * ks[1],
            vs[0] * ks[0], vs[1] * ks[0], vs[0] * ks[1], vs[1] * ks[1],
        )

    acc_first = sum_chunks(7, chunk_first)
    fill_strip(1, v)
    round_strip(1)

    def chunk_bent(s, r0):
        bend_rows(v, s, r0)
        vs = pair_of(v, s, r0)
        curved, along = columns(vs, seconds, nexts)
        ks = stiff(vs, bends_of(curved, s, r0), s, r0)
        ahead = ahead_of(v, vs, s, r0)
        for i in range(2):
            colv[i, flat(s, r0), :] = along[i]
            rowv[i, flat(s, r0), :] = ahead[i]
            kv[i, flat(s, r0), :] = ks[i]
        return vs[0] * ks[0], vs[0] * ks[1], vs[1] * ks[1]

    acc_bent = sum_chunks(3, chunk_bent)

    own_ids.wait()
    all_ids().wait_recv()
    who = jnp.broadcast_to(ids[...], (n, per_peer, LANES)).reshape(rows_dev, LANES)
    wide_lane = lax.broadcasted_iota(jnp.int32, (rows_dev, LANES), 1)
    wide_row = lax.broadcasted_iota(jnp.int32, (rows_dev, LANES), 0)
    pick = wide_lane == lax.rem(me * per_peer, LANES) + lax.rem(wide_row, per_peer)
    target = lax.rem(
        jnp.sum(jnp.where(pick, who, 0).astype(jnp.float32), axis=1, keepdims=True).astype(jnp.int32),
        rows_dev,
    )
    to = lax.broadcasted_iota(jnp.int32, (rows_dev, rows_dev), 1)
    onehot[...] = jnp.transpose((to == target).astype(jnp.float32)).astype(jnp.bfloat16)

    own_data.wait()
    all_data().wait_recv()
    second_strips = along_patch(high.at[0], got_high.at[0], high_send.at[0], high_recv.at[0], everyone)
    for copy in second_strips:
        copy.start()
    for c in range(3):
        block = arrived[c]
        if per_peer % 8:
            block = block.astype(jnp.float32).reshape(rows_dev, ncol).astype(jnp.bfloat16)
        else:
            block = block.reshape(rows_dev, ncol)
        stress[c] = jnp.dot(onehot[...], block, preferred_element_type=jnp.float32)

    first_spot = lax.broadcasted_iota(jnp.int32, (1, ncol), 1) == 0

    def fill_edges():
        for s in range(slots):
            length = jnp.maximum(lengths[s], 3)
            for i in range(2):
                def line(ref, k, r):
                    return ref[k, pl.ds(s * prows + r, 1), :]

                def flux(r):
                    return line(stress, 0, r) * line(rowx, i, r) + line(stress, 2, r) * line(colx, i, r)

                def value(r, lower):
                    across = line(stress, 1, r) * line(colx, i, r) + line(stress, 2, r) * line(rowx, i, r)
                    back = jnp.where(first_spot, 0.0, pltpu.roll(across, 1, 1)) - across
                    return prec[pl.ds(s * prows + r, 1), :] * (lower - flux(r) + back)

                at = i * slots + s
                last = value(length - 1, flux(length - 2))
                ahead = value(length - 2, flux(length - 3))
                first = value(0, 0.0)
                second = value(1, flux(0))
                strips[2, at : at + 1, :] = last
                strips[2, group + at : group + at + 1, :] = last - ahead
                strips[2, side + at : side + at + 1, :] = first
                strips[2, side + group + at : side + group + at + 1, :] = second - first

    fill_edges()
    round_strip(2)
    third_strips = along_patch(high.at[1], got_high.at[1], high_send.at[1], high_recv.at[1], everyone)
    low_strips = [
        copy
        for k in range(2)
        for copy in along_patch(low.at[k], got_low.at[k], low_send.at[k], low_recv.at[k], beside)
    ]
    for copy in third_strips + low_strips:
        copy.start()

    def chunk_stress(s, r0):
        at = flat(s, r0)
        _, across = flows_of(*(both_of(ref, at) for ref in (rowx, colx)), s, r0, frow)
        gs = geometric(across, s, r0, frow)
        for i in range(2):
            gf[i, at, :] = gs[i]
            place(w, i, s, r0, prec[at, :] * gs[i])
        x0, x1 = pair_of(x, s, r0)
        return x0 * gs[0], x0 * gs[1], x1 * gs[1]


    def chunk_second(s, r0):
        at = flat(s, r0)
        ws = pair_of(w, s, r0)
        curved, along = columns(ws, seconds, nexts)
        ahead = ahead_of(w, ws, s, r0)
        kept, across = flows_of(ahead, along, s, r0, frow)
        ahead_v, along_v = both_of(rowv, at), both_of(colv, at)
        kept_v, across_v = flows_of(ahead_v, along_v, s, r0, fside)
        bends = bends_of(curved, s, r0)
        fo = found[at, :]
        th = thick[at, :]
        live = live_rows(s, r0)
        arches = [rows(w, i, s, r0, -1) - 2.0 * ws[i] + rows(w, i, s, r0, 1) for i in range(2)]
        arch_live = [jnp.where(live, th * arch, 0.0) for arch in arches]
        for i in range(2):
            place(mrow, i, s, r0, arch_live[i])
            fa[i, at, :] = across[i]
            fb[i, at, :] = across_v[i]
            fc[i, at, :] = bends[i]
        gs, ks, kvs = both_of(gf, at), both_of(kf, at), both_of(kv, at)
        pairs = ((0, 0), (0, 1), (1, 1))
        squares = ((0, 0), (0, 1), (1, 0), (1, 1))
        held = [fo * field for field in ws]
        return (
            *(ws[i] * gs[j] for i, j in pairs),
            *(ws[i] * ks[j] for i, j in squares),
            *(ahead[i] * kept[j] + along[i] * across[j] for i, j in pairs),
            *(ahead_v[j] * kept[i] + along_v[j] * across[i] for i, j in squares),
            *(ahead_v[i] * kept_v[j] + along_v[i] * across_v[j] for i, j in pairs),
            *(held[i] * ws[j] + bends[i] * curved[j] + arch_live[i] * arches[j] for i, j in pairs),
            *(ws[i] * kvs[j] for i, j in squares),
        )

    def chunk_both(s, r0):
        ahead_of_w = chunk_stress(s, r0)
        return *ahead_of_w, *chunk_second(s, r0)

    acc = sum_chunks(27, chunk_both)
    acc_stress, acc = acc[:3], acc[3:]
    last = [a + b for a, b in zip(acc[20:], acc_first[3:])]
    values = [*acc_first[:3], *acc_bent, *acc_stress, *acc[:20], *last]
    sums[me] = to_line(values, range(len(values)))

    def send_line(k, where):
        pltpu.make_async_remote_copy(
            src_ref=sums.at[me], dst_ref=sums.at[me], send_sem=sum_send.at[0],
            recv_sem=sum_recv.at[0], device_id=where, device_id_type=MESH,
        ).start()

    for_peers(send_line)

    for copy in second_strips:
        copy.wait_recv()
    labels = {d: label_of(d) for d in range(owners)}
    v_jumps = [jumps(1, d, labels[d], False) for d in range(owners)]
    for copy in third_strips:
        copy.wait_recv()
    weight = jnp.where(strip_row < group, penalty_value, penalty_slope)
    forms = None
    for d in range(owners):
        w_jump, v_jump = jumps(2, d, labels[d], False), v_jumps[d]
        scaled = weight * w_jump
        scaled_v = weight * v_jump
        terms = [
            scaled * w_jump, scaled * pltpu.roll(w_jump, slots, 0),
            scaled * v_jump, scaled * pltpu.roll(v_jump, slots, 0),
            scaled * pltpu.roll(v_jump, side - slots, 0),
            scaled_v * v_jump, scaled_v * pltpu.roll(v_jump, slots, 0),
        ]
        forms = terms if forms is None else [a + b for a, b in zip(forms, terms)]
    half_rows = lax.rem(lax.broadcasted_iota(jnp.int32, (side, LANES), 0), group) < slots
    spots, values = [], []
    for t, form, first in (
        (26, 0, True), (27, 1, False), (28, 0, False),
        (29, 2, True), (30, 4, True), (31, 3, False), (32, 2, False),
        (3, 5, True), (4, 6, False), (5, 5, False),
    ):
        value = forms[form][:, 0:LANES]
        for j in range(LANES, ncol, LANES):
            value = value + forms[form][:, j : j + LANES]
        spots.append(t)
        values.append(jnp.where(half_rows, value, 0.0) if first else jnp.where(half_rows, 0.0, value))
    line = to_line(values, spots)
    spot_of = si * halves + hi
    joints[spot_of] = line
    joint_copies = []
    for e in range(1, subs * halves):
        joint_copies.append(
            pltpu.make_async_remote_copy(
                src_ref=joints.at[spot_of], dst_ref=joints.at[spot_of],
                send_sem=joint_send.at[e - 1], recv_sem=joint_recv.at[e - 1],
                device_id={
                    "sub": lax.rem(si + e // halves, subs), "half": lax.rem(hi + e % halves, halves)
                },
                device_id_type=MESH,
            )
        )
    for copy in joint_copies:
        copy.start()

    for copy in low_strips:
        copy.wait_recv()
    for which in (1, 2):
        set_edges(which, jumps(which, 0, labels[0], True), jumps_below(which, labels))

    @for_chunks
    def _(s, r0):
        at = flat(s, r0)
        p = prec[at, :]
        xs, ws, vs = (pair_of(ref, s, r0) for ref in (x, w, v))
        kw = stiff(ws, both_of(fc, at), s, r0)
        gw = geometric(both_of(fa, at), s, r0, frow)
        gv = geometric(both_of(fb, at), s, r0, fside)
        for i in range(2):
            fa[i, at, :] = xs[i] + 2.0 * ws[i] + p * gw[i]
            fb[i, at, :] = vs[i] + p * gv[i]
            fc[i, at, :] = vs[i] + p * (kw[i] + joint(2, i, s, r0))
            fd[i, at, :] = p * (kv[i, at, :] + joint(1, i, s, r0))

    all_sums().wait_recv()
    line = jnp.sum(sums[...], axis=0)
    lanes = [line[:, t : t + 1] for t in range(33)]
    a1, c, a2, pk0, pk1, pk2, g1, h, g2 = lanes[:9]
    wg, wk, ww, wv, vv, kww = lanes[9:12], lanes[12:16], lanes[16:19], lanes[19:23], lanes[23:26], lanes[26:29]
    uk = (a1 + 2.0 * wk[0] + kww[0], c + wk[1] + wk[2] + kww[1], a2 + 2.0 * wk[3] + kww[2])
    ug = tuple(g + 2.0 * b + q for g, b, q in zip((g1, h, g2), wg, ww))
    mixed_g = tuple(b + q for b, q in zip(wk, wv))

    def ratios(a1, c, a2, g1, h, g2):
        ratio = c / a1
        other_a = a2 - ratio * c
        other_q = g2 - 2.0 * ratio * h + ratio * ratio * g1
        return (
            ratio, g1 / a1, other_q / other_a,
            jnp.sqrt(norm_scale * cells / a1), jnp.sqrt(norm_scale * cells / other_a),
        )

    r, mu1, mu2, s0, s1 = ratios(a1, c, a2, g1, h, g2)

    def stepped(uu, uv, vv):
        uu0, uu1, uu2 = uu
        uv00, uv01, uv10, uv11 = uv
        vv0, vv1, vv2 = vv
        uu2 = uu2 - 2.0 * r * uu1 + r * r * uu0
        uu1 = uu1 - r * uu0
        uv11 = uv11 - r * (uv10 + uv01) + r * r * uv00
        uv01 = uv01 - r * uv00
        uv10 = uv10 - r * uv00
        vv2 = vv2 - 2.0 * r * vv1 + r * r * vv0
        vv1 = vv1 - r * vv0
        first = s0 * s0 * (uu0 - 2.0 * mu1 * uv00 + mu1 * mu1 * vv0)
        cross = s0 * s1 * (uu1 - mu2 * uv01 - mu1 * uv10 + mu1 * mu2 * vv1)
        second = s1 * s1 * (uu2 - 2.0 * mu2 * uv11 + mu2 * mu2 * vv2)
        return first, cross, second

    next_g = stepped(ug, mixed_g, vv)
    next_a = stepped(uk, lanes[29:33], (pk0, pk1, pk2))
    for copy in joint_copies:
        copy.wait_recv()
    line = jnp.sum(joints[...], axis=0)
    parts = [line[:, t : t + 1] for t in (*range(26, 33), *range(3, 6))]
    next_a = tuple(a + b for a, b in zip(next_a, stepped(parts[:3], parts[3:7], parts[7:])))
    r2, nu1, nu2, t0, t1 = ratios(*next_a, *next_g)
    e1 = t0 * s0
    f1 = t1 * s1
    f5 = -t1 * (s1 * r + r2 * s0)
    f6 = t1 * (s1 * r * mu2 + r2 * s0 * mu1)
    values = (
        e1, -e1 * mu1, -e1 * nu1, e1 * mu1 * nu1,
        f1, -f1 * mu2, -f1 * nu2, f1 * mu2 * nu2,
        f5, f6, -nu2 * f5, -nu2 * f6,
    )
    for t, value in enumerate(values):
        coef[t : t + 1, :] = jnp.broadcast_to(value, (1, ncol))

    for copy in first_strips + name_copies + second_strips + third_strips + low_strips + joint_copies:
        copy.wait_send()
    all_ids().wait_send()
    all_data().wait_send()
    all_sums().wait_send()


def combine(fa, fb, fc, fd, coef, out, both, sem):
    rows_dev = fa.shape[1]
    piece = rows_dev // 8
    copies = []
    for k in range(8):
        at = pl.ds(k * piece, piece)
        firsts = [ref[0, at, :] for ref in (fa, fb, fc, fd)]
        seconds = [ref[1, at, :] for ref in (fa, fb, fc, fd)]

        def mixed(first, fields):
            total = coef[first : first + 1, :] * fields[0]
            for t, field in enumerate(fields[1:], first + 1):
                total = total + coef[t : t + 1, :] * field
            return total

        both[0, at, :] = mixed(0, firsts)
        both[1, at, :] = mixed(4, seconds + firsts)
        copy = pltpu.make_async_copy(both.at[:, at], out.at[:, at], sem.at[k])
        copy.start()
        copies.append(copy)
    for copy in copies:
        copy.wait()


def per_device(vectors, prestress, thickness, foundation, patch_rows, matched, elem_row):
    n = lax.axis_size(("patch", "sub", "half"))
    owners = lax.axis_size("patch")
    inner = n // owners
    slots = patch_rows.shape[0]
    rows_dev, ncol = thickness.shape
    prows = rows_dev // slots
    per_peer = rows_dev // n
    pre = jnp.transpose(prestress, (1, 0, 2)).reshape(3, n, per_peer, ncol)
    elem = elem_row.reshape(rows_dev // LANES, 1, LANES)
    f32 = jnp.float32
    padded = pltpu.VMEM((2, slots, prows + 2 * PAD, ncol), f32)
    flat = pltpu.VMEM((rows_dev, ncol), f32)
    pair = pltpu.VMEM((2, rows_dev, ncol), f32)
    side = 4 * slots
    hbm = pl.BlockSpec(memory_space=pltpu.HBM)
    dma = pltpu.SemaphoreType.DMA
    operands = (vectors, pre, thickness, foundation, patch_rows, matched, elem)
    in_vmem = pl.BlockSpec(memory_space=pltpu.VMEM)
    field = jax.ShapeDtypeStruct((2, rows_dev, ncol), f32)
    parts = pl.pallas_call(
        body,
        out_shape=[field] * 4 + [jax.ShapeDtypeStruct((16, ncol), f32)],
        in_specs=[hbm] * 7,
        out_specs=[in_vmem] * 5,
        scratch_shapes=[
            pltpu.SMEM((slots,), jnp.int32), pltpu.SMEM((slots,), jnp.int32),
            padded, padded, padded, padded, padded, padded, flat, flat, flat,
            pltpu.VMEM((3, rows_dev, ncol), f32),
            pair, pair, pair, pair, pair, pair, pair,
            pltpu.VMEM((2 * ncol, ncol), jnp.bfloat16),
            pltpu.VMEM((2 * ncol, ncol), jnp.bfloat16),
            pltpu.VMEM((3, n, per_peer, ncol), jnp.bfloat16),
            pltpu.VMEM((n, 1, LANES), jnp.int32),
            pltpu.VMEM((rows_dev, rows_dev), jnp.bfloat16),
            pltpu.VMEM((3, 2 * side, ncol), f32),
            pltpu.VMEM((owners - 1, 2 * side, ncol), f32),
            pltpu.VMEM((2, 2 * side, ncol), jnp.bfloat16),
            pltpu.VMEM((2, owners - 1, 2 * side, ncol), jnp.bfloat16),
            pltpu.VMEM((2, 2 * side, ncol), jnp.bfloat16),
            pltpu.VMEM((2, owners - 1, 2 * side, ncol), jnp.bfloat16),
            pltpu.VMEM((owners, 1, LANES), f32),
            pltpu.VMEM((3, 2 * side, ncol), f32),
            pltpu.VMEM((n, 1, LANES), f32),
            pltpu.VMEM((inner, 1, LANES), f32),
            dma((2 * slots + 2,)), dma((4,)),
            dma((1,)), dma((1,)), dma((1,)), dma((1,)),
            dma((owners - 1,)), dma((owners - 1,)),
            dma((2, owners - 1)), dma((2, owners - 1)),
            dma((2, owners - 1)), dma((2, owners - 1)),
            dma((owners - 1,)), dma((owners - 1,)),
            dma((1,)), dma((1,)), dma((inner - 1,)), dma((inner - 1,)),
        ],
        compiler_params=pltpu.CompilerParams(
            collective_id=0, has_side_effects=True, vmem_limit_bytes=32 << 20
        ),
    )(*(pltpu.with_memory_space_constraint(a, pltpu.HBM) for a in operands))
    return pl.pallas_call(
        combine,
        out_shape=field,
        in_specs=[in_vmem] * 5,
        out_specs=hbm,
        scratch_shapes=[pair, dma((8,))],
        compiler_params=pltpu.CompilerParams(vmem_limit_bytes=8 << 20),
    )(*parts)


def solution(mesh):
    split = ("groups", "patch", "sub", "half")
    in_specs = (
        P(None, split, None),
        P(split, None, None),
        P(split, None),
        P(split, None),
        P(split),
        P(split),
        P(split),
    )
    return jax.shard_map(
        per_device, mesh=mesh, in_specs=in_specs, out_specs=P(None, split, None), check_vma=False
    )
```
